512 devices in a mesh: tok: 64 (over z_hi, x, y), tp: 8 (over z_lo, core).
Axes of the slice: x: 4, y: 8, z: 8 (z_hi: 2, z_lo: 4; z = z_hi * 4 + z_lo), core: 2. Of those that a mesh axis runs over, the one named last changes fastest.
Arguments:
- tokens: bfloat16 [8192, 4096], P('tok', 'tp'), may hold values from -6 to 6
- w_query: bfloat16 [4096, 4096], P('tok', 'tp'), may hold values from -0.09375 to 0.09375
- w_key: bfloat16 [4096, 4096], P('tok', 'tp'), may hold values from -0.09375 to 0.09375
- w_value: bfloat16 [4096, 4096], P('tok', 'tp'), may hold values from -0.09375 to 0.09375
- short_taps: float32 [3, 3, 4096], P(None, None, 'tp'), may hold values from -3.5 to 3.5
- filters: float32 [4096, 8192], P(('tp', 'tok')), may hold values from -90 to 90, as said below
- skip_gain: float32 [4096], P(('tp', 'tok')), may hold values from 0.1 to 1.9
Outputs:
- layer_out: bfloat16 [8192, 4096], P('tok', 'tp')
The draws below stay inside these ranges and needn't reach their ends.
Inputs may be any that keep to these rules, and one draw needn't show every extreme that they name: `filters`: real-valued filter taps.
All inputs are finite; a program needn't handle non-finite values.
Results may differ from the reference program's by a relative error of at most 0.009.
Values may be sent and summed in bfloat16 or wider, within the bound.
No kernel may reach another device: no remote copies, remote signals or barrier semaphores. Data moves between devices by JAX's collectives and lax.ppermute only.
A program may use at most 64 MiB of HBM per device.

```python
import math
import jax
import jax.numpy as jnp
from jax import lax

D = 4096
SEQ = 8192


def draw_filters(key, part):
    first, second, third, fourth = jax.random.split(key, 4)
    base = jnp.clip(jax.random.normal(first, (D, SEQ), jnp.float32), -6.0, 6.0)
    channel = jnp.exp(jax.random.uniform(second, (D, 1), jnp.float32, 0.0, math.log(10.0)))
    rough = jax.random.uniform(third, (1, SEQ), jnp.float32, 0.5, 1.5)
    rate = jax.random.uniform(fourth, (D, 1), jnp.float32, 0.0, 3.0)
    place = jnp.arange(SEQ, dtype=jnp.float32)[None, :] / SEQ
    return base * channel * rough * jnp.exp(-rate * place)


def block_scale(key, dims, shards, low, top_value):
    def one(dim, shards_of):
        draws = jax.random.uniform(jax.random.fold_in(jax.random.fold_in(key, 6), dim), (shards_of,), jnp.float32, low / len(shards), top_value / len(shards))
        return jnp.repeat(jnp.exp(draws), dims[dim] // shards_of).reshape((-1,) + (1,) * (len(dims) - dim - 1))

    loudness = one(*shards[0])
    for cut in shards[1:]:
        loudness = loudness * one(*cut)
    return loudness


def bell_draw(stream_key, dims, scale, reach, cuts=(), kind=jnp.bfloat16):
    factor_of = block_scale(stream_key, dims, cuts, -0.22, 0.18) if cuts else 1.0
    entries = jax.random.normal(stream_key, dims, jnp.float32) * scale * factor_of
    return jnp.minimum(jnp.maximum(entries, -reach), reach).astype(kind)


def setup_inputs(seed: int = 0) -> dict:
    seeds = jax.random.split(jax.random.key(seed), 8)
    tokens = bell_draw(seeds[0], (SEQ, D), 1.0, 6.0, ((0, 64), (1, 8)))
    w_query = bell_draw(seeds[1], (D, D), D ** -0.5, 0.09375, ((0, 64), (1, 8)))
    w_key = bell_draw(seeds[2], (D, D), D ** -0.5, 0.09375, ((0, 64), (1, 8)))
    w_value = bell_draw(seeds[3], (D, D), D ** -0.5, 0.09375, ((0, 64), (1, 8)))
    short_taps = bell_draw(seeds[4], (3, 3, D), 3 ** -0.5, 3.5, ((2, 8),), jnp.float32)
    filters = draw_filters(jax.random.fold_in(seeds[7], 71), 0)
    skip_gain = jnp.clip(1.0 + 0.18 * jax.random.normal(seeds[6], (D,), jnp.float32), 0.1, 1.9)
    return dict(tokens=tokens, w_query=w_query, w_key=w_key, w_value=w_value, short_taps=short_taps, filters=filters, skip_gain=skip_gain)


def short_conv(raw, taps):
    padded = jnp.pad(raw, ((2, 0), (0, 0)))
    return taps[0][None, :] * raw + taps[1][None, :] * padded[1:-1] + taps[2][None, :] * padded[:-2]

def reference(tokens, w_query, w_key, w_value, short_taps, filters, skip_gain):
    query_raw = jnp.dot(tokens, w_query, preferred_element_type=jnp.float32)
    query = short_conv(query_raw, short_taps[0]).astype(jnp.bfloat16)
    query = lax.optimization_barrier(query)
    keyed = short_conv(jnp.dot(tokens, w_key, preferred_element_type=jnp.float32), short_taps[1])
    valued = short_conv(jnp.dot(tokens, w_value, preferred_element_type=jnp.float32), short_taps[2])
    key_value = (keyed * valued).astype(jnp.bfloat16)
    key_value = lax.optimization_barrier(key_value)
    length = tokens.shape[0]
    signal = key_value.astype(jnp.float32).T
    width = signal.shape[0]
    block = math.gcd(width, 256)

    def convolve(pair):
        series, taps = pair
        unit = taps / jnp.sqrt(lax.optimization_barrier(jnp.sum(taps * taps, axis=1, keepdims=True)) + 1e-06)
        spectrum = jnp.fft.rfft(series, n=2 * length, axis=1) * jnp.fft.rfft(unit, n=2 * length, axis=1)
        return jnp.fft.irfft(spectrum, n=2 * length, axis=1)[:, :length]
    convolved = lax.map(convolve, (signal.reshape(width // block, block, length), filters.reshape(width // block, block, length)))
    convolved = convolved.reshape(width, length)
    mixed = (convolved + skip_gain[:, None] * signal).astype(jnp.bfloat16)
    mixed = lax.optimization_barrier(mixed)
    return (query.astype(jnp.float32) * mixed.T.astype(jnp.float32)).astype(jnp.bfloat16)
```

```python
import functools
import math

import jax
import jax.numpy as jnp
import numpy as np
from jax import lax
from jax.experimental import pallas as pl
from jax.experimental.pallas import tpu as pltpu
from jax.sharding import Mesh
from jax.sharding import PartitionSpec as P

AXES = ("z_hi", "x", "yh", "yl", "z_lo", "core")
SIZES = (2, 4, 4, 2, 4, 2)
TOK = AXES[:4]
TP = AXES[4:]
HALO = 8
BLOCK = 128
ROWS = HALO + BLOCK
POINTS = 128
F32 = jnp.float32
BF16 = jnp.bfloat16


def exchanged(value, axes):
    return lax.all_to_all(value, axes, split_axis=0, concat_axis=0, tiled=True)


def from_everyone(value, axes):
    count = math.prod(SIZES[AXES.index(a)] for a in axes)
    return exchanged(jnp.broadcast_to(value, (count, *value.shape)), axes)


def dft_tables():
    n = np.arange(POINTS)
    full = 2.0 * np.pi * (np.outer(n, n) % POINTS) / POINTS
    cos, sin = np.cos(full), np.sin(full)
    half = POINTS // 2
    outer = np.concatenate([cos[:, :half], -sin[:, :half]], axis=0)
    inner = np.block([[cos, -sin], [sin, cos]])
    back_inner = np.block([[cos, sin], [-sin, cos]])
    back_outer = np.concatenate([cos[:half], -sin[:half]], axis=1) / POINTS**2
    twist = 2.0 * np.pi * np.outer(n, n) / POINTS**2
    as_bf16 = lambda a: jnp.asarray(a, F32).astype(BF16)
    return (
        as_bf16(outer),
        as_bf16(inner),
        as_bf16(back_inner),
        as_bf16(back_outer),
        jnp.asarray(np.cos(twist), F32),
        jnp.asarray(np.sin(twist), F32),
    )


def dot(a, b):
    return jnp.dot(a, b, preferred_element_type=F32)


def spectrum(rows, outer, inner, cos, sin):
    blocks = jnp.concatenate(
        [rows[pl.ds(c, 64, stride=8), :].astype(BF16) for c in range(8)], axis=1
    )
    first = dot(outer, blocks)
    turned = []
    for c in range(8):
        re = first[:POINTS, c * POINTS : (c + 1) * POINTS]
        im = first[POINTS:, c * POINTS : (c + 1) * POINTS]
        turned.append(
            jnp.concatenate([re * cos + im * sin, im * cos - re * sin], axis=1).astype(BF16)
        )
    return dot(jnp.concatenate(turned, axis=0), inner)


def filter_kernel(filters, outer, inner, cos, sin, spec, rows):
    taps = filters[...]
    unit = taps / jnp.sqrt(jnp.sum(taps * taps, axis=1, keepdims=True) + 1e-06)
    for b in range(64):
        rows[pl.ds(b * 8, 8), :] = unit[:, b * POINTS : (b + 1) * POINTS]
    spec[...] = spectrum(rows, outer[...], inner[...], cos[...], sin[...])


def conv_kernel(signal, spec, skip, outer, inner, back_inner, back_outer, cos, sin, mixed, rows, out):
    for z in range(2):
        rows[pl.ds(z * 256, 256), :] = signal[:, z].astype(F32).reshape(256, POINTS)
    cos_t, sin_t = cos[...], sin[...]
    sig = spectrum(rows, outer[...], inner[...], cos_t, sin_t)
    re, im = sig[:, :POINTS], sig[:, POINTS:]
    f_re, f_im = spec[:, :POINTS], spec[:, POINTS:]
    prod = jnp.concatenate([re * f_re - im * f_im, re * f_im + im * f_re], axis=1)
    back = dot(prod.astype(BF16), back_inner[...])
    turned = []
    for c in range(8):
        b_re = back[c * POINTS : (c + 1) * POINTS, :POINTS]
        b_im = back[c * POINTS : (c + 1) * POINTS, POINTS:]
        turned.append(
            jnp.concatenate([b_re * cos_t - b_im * sin_t, b_re * sin_t + b_im * cos_t], axis=0).astype(BF16)
        )
    result = dot(back_outer[...], jnp.concatenate(turned, axis=1))
    for c in range(8):
        piece = result[:, c * POINTS : (c + 1) * POINTS]
        out[pl.ds(c, 64, stride=8), :] = piece + skip[c] * rows[pl.ds(c, 64, stride=8), :]
    mixed[...] = out[...].astype(BF16).reshape(64, 8, POINTS)


def order_table(rows_are_natural):
    shape = (512, 512)
    row = lax.broadcasted_iota(jnp.int32, shape, 0)
    col = lax.broadcasted_iota(jnp.int32, shape, 1)
    grouped, natural = (col, row) if rows_are_natural else (row, col)
    z_hi, yl, xy, j = grouped // 256, (grouped // 128) % 2, (grouped // 8) % 16, grouped % 8
    return (natural == z_hi * 256 + xy * 16 + yl * 8 + j).astype(F32).astype(BF16)


def weights_kernel(w_key, w_value, w_query, out):
    table = order_table(True)
    for p, ref in enumerate((w_key, w_value, w_query)):
        sorted_cols = dot(ref[...], table).astype(BF16)
        for quarter in range(4):
            piece = sorted_cols[:, quarter * 128 : (quarter + 1) * 128]
            for yh in range(4):
                out[quarter // 2, yh, quarter % 2, :, p * 128 : (p + 1) * 128] = piece


def projected(x, w, at, width, acc):
    for tp in range(8):
        z_lo, core = tp // 2, tp % 2
        z_hi, col = tp // 4, tp % 4
        rows = x[core, z_lo].reshape(4 * ROWS, 512)
        weights = w[col, z_hi, :, :, at : at + width].reshape(512, width)
        term = dot(rows, weights)
        if tp == 0:
            acc[...] = term
        else:
            acc[...] += term


def short(acc, group, at, taps):
    top = group * ROWS + HALO
    cols = pl.ds(at, 128)
    return (
        taps[0:1] * acc[pl.ds(top, BLOCK), cols]
        + taps[1:2] * acc[pl.ds(top - 1, BLOCK), cols]
        + taps[2:3] * acc[pl.ds(top - 2, BLOCK), cols]
    )


def key_value_kernel(x, w, taps, out, acc):
    projected(x, w, 0, 256, acc)
    for group in range(4):
        keyed = short(acc, group, 0, taps[1])
        valued = short(acc, group, 128, taps[2])
        out[:, group] = (keyed * valued).T.reshape(16, 8, BLOCK).astype(BF16)


def query_kernel(x, w, taps, out, acc):
    projected(x, w, 256, 128, acc)
    for group in range(4):
        out[group] = short(acc, group, 0, taps[0]).astype(BF16)


def gate_kernel(query, returned, out):
    cols = jnp.concatenate([query[g] for g in range(4)], axis=1)
    natural = dot(cols, order_table(False))
    mixed = returned[...].astype(F32).reshape(512, BLOCK).T
    out[...] = (natural * mixed).astype(BF16)


def call(kernel, shape, dtype, args, scratch=(), in_specs=None, flops=10**8, name=None):
    whole = pl.BlockSpec(memory_space=pltpu.VMEM)
    specs = in_specs or [whole] * len(args)
    moved = sum(math.prod(a.shape) * a.dtype.itemsize for a in args)
    return pl.pallas_call(
        kernel,
        out_shape=jax.ShapeDtypeStruct(shape, dtype),
        in_specs=specs,
        out_specs=whole,
        scratch_shapes=list(scratch),
        compiler_params=pltpu.CompilerParams(vmem_limit_bytes=48 * 2**20),
        cost_estimate=pl.CostEstimate(flops=flops, bytes_accessed=moved, transcendentals=0),
        name=name,
    )(*args)


def local(tokens, w_query, w_key, w_value, short_taps, filters, skip_gain):
    count = math.prod(SIZES[:4])
    halo = lax.ppermute(tokens[-HALO:], TOK, [(i, i + 1) for i in range(count - 1)])

    sent = call(weights_kernel, (2, 4, 2, 64, 384), BF16, (w_key, w_value, w_query), name="sort_weights")
    first = exchanged(sent.reshape(16, 64, 384), ("z_hi", "yh", "yl"))
    weights = from_everyone(first, ("x",)).reshape(4, 2, 8, 64, 384)

    extended = jnp.concatenate([halo, tokens], axis=0)
    part = from_everyone(extended, ("z_lo", "z_hi", "yl"))
    features = from_everyone(part.reshape(4, 4, ROWS, 512), ("core",)).reshape(2, 4, 4, ROWS, 512)

    z_hi, yl = lax.axis_index("z_hi"), lax.axis_index("yl")
    taps = short_taps.reshape(3, 3, 2, 16, 2, 8)
    taps = lax.dynamic_index_in_dim(taps, z_hi, 2, keepdims=False)
    taps = lax.dynamic_index_in_dim(taps, yl, 3, keepdims=False).reshape(3, 3, 128)

    outer, inner, back_inner, back_outer, cos, sin = dft_tables()
    spec = call(
        filter_kernel,
        (8 * POINTS, 2 * POINTS),
        F32,
        (filters, outer, inner, cos, sin),
        (pltpu.VMEM((512, POINTS), F32),),
        name="filter_spectrum",
    )

    whole = pl.BlockSpec(memory_space=pltpu.VMEM)
    key_value = call(
        key_value_kernel,
        (16, 4, 8, BLOCK),
        BF16,
        (features, weights, taps),
        (pltpu.VMEM((4 * ROWS, 256), F32),),
        flops=2 * 544 * 4096 * 256,
        name="key_value",
    )
    owned = exchanged(key_value, ("x", "yh"))
    query = call(
        query_kernel,
        (4, BLOCK, 128),
        BF16,
        (features, weights, taps),
        (pltpu.VMEM((4 * ROWS, 128), F32),),
        flops=2 * 544 * 4096 * 128,
        name="query",
    )
    query = exchanged(query, ("z_hi", "yl"))
    smem = pl.BlockSpec(memory_space=pltpu.SMEM)
    mixed = call(
        conv_kernel,
        (64, 8, BLOCK),
        BF16,
        (owned.reshape(16, 2, 2, 8, BLOCK), spec, skip_gain, outer, inner, back_inner, back_outer, cos, sin),
        (pltpu.VMEM((512, POINTS), F32), pltpu.VMEM((512, POINTS), F32)),
        in_specs=[whole, whole, smem] + [whole] * 6,
        flops=2 * 168 * 10**6,
        name="long_conv",
    )
    returned = exchanged(mixed, TOK)
    return call(gate_kernel, (BLOCK, 512), BF16, (query, returned), name="gate")


def solution(mesh):
    fine = Mesh(mesh.devices.reshape(SIZES), AXES)
    in_specs = (
        P(TOK, TP),
        P(TOK, TP),
        P(TOK, TP),
        P(TOK, TP),
        P(None, None, TP),
        P(TP + TOK, None),
        P(TP + TOK),
    )
    return jax.shard_map(local, mesh=fine, in_specs=in_specs, out_specs=P(TOK, TP), check_vma=False)
```

```python
import math

import jax
import jax.numpy as jnp
import numpy as np
from jax import lax
from jax.experimental import pallas as pl
from jax.experimental.pallas import tpu as pltpu
from jax.sharding import Mesh
from jax.sharding import PartitionSpec as P

AXES = ("z_hi", "x", "yh", "yl", "z_lo", "core")
SIZES = (2, 4, 4, 2, 4, 2)
TOK = AXES[:4]
TP = AXES[4:]
HALO = 8
BLOCK = 128
ROWS = HALO + BLOCK
POINTS = 128
F32 = jnp.float32
BF16 = jnp.bfloat16


def exchanged(value, axes):
    return lax.all_to_all(value, axes, split_axis=0, concat_axis=0, tiled=True)


def from_everyone(value, axes):
    count = math.prod(SIZES[AXES.index(a)] for a in axes)
    return exchanged(jnp.broadcast_to(value, (count, *value.shape)), axes)


def dft_tables():
    n = np.arange(POINTS)
    full = 2.0 * np.pi * (np.outer(n, n) % POINTS) / POINTS
    cos, sin = np.cos(full), np.sin(full)
    half = POINTS // 2
    outer = np.concatenate([cos, -sin], axis=0)
    outer = np.concatenate([outer, outer], axis=1)
    inner = np.block([[cos, -sin], [sin, cos]])
    back_inner = np.block([[cos, sin], [-sin, cos]])
    back_outer = np.concatenate([cos[:half], -sin[:half]], axis=1) / POINTS**2
    twist = 2.0 * np.pi * np.outer(n, n) / POINTS**2
    tables = np.concatenate([inner, back_inner, outer, back_outer], axis=0)
    turns = np.concatenate([np.cos(twist), np.sin(twist)], axis=0)
    return jnp.asarray(tables, F32).astype(BF16), jnp.asarray(turns, F32)


def dot(a, b):
    return jnp.dot(a, b, preferred_element_type=F32)


def spectrum(rows, tables, turns):
    cos, sin = turns[0:POINTS], turns[POINTS:]
    blocks = jnp.concatenate(
        [rows[pl.ds(c, 64, stride=8), :].astype(BF16) for c in range(8)], axis=1
    )
    first = dot(tables[512:768, 0:64], blocks)
    turned = []
    for c in range(8):
        re = first[:POINTS, c * POINTS : (c + 1) * POINTS]
        im = first[POINTS:, c * POINTS : (c + 1) * POINTS]
        turned.append(
            jnp.concatenate([re * cos + im * sin, im * cos - re * sin], axis=1).astype(BF16)
        )
    return dot(jnp.concatenate(turned, axis=0), tables[0:256])


def filter_kernel(filters, tables, turns, spec, rows):
    taps = filters[...]
    unit = taps / jnp.sqrt(jnp.sum(taps * taps, axis=1, keepdims=True) + 1e-06)
    for b in range(64):
        rows[pl.ds(b * 8, 8), :] = unit[:, b * POINTS : (b + 1) * POINTS]
    spec[...] = spectrum(rows, tables, turns)


def conv_kernel(signal, spec, skip, tables, turns, mixed, rows, out):
    for z in range(2):
        rows[pl.ds(z * 256, 256), :] = signal[:, z].astype(F32).reshape(256, POINTS)
    cos, sin = turns[0:POINTS], turns[POINTS:]
    sig = spectrum(rows, tables, turns)
    re, im = sig[:, :POINTS], sig[:, POINTS:]
    f_re, f_im = spec[:, :POINTS], spec[:, POINTS:]
    prod = jnp.concatenate([re * f_re - im * f_im, re * f_im + im * f_re], axis=1)
    back = dot(prod.astype(BF16), tables[256:512])
    turned = []
    for c in range(8):
        b_re = back[c * POINTS : (c + 1) * POINTS, :POINTS]
        b_im = back[c * POINTS : (c + 1) * POINTS, POINTS:]
        turned.append(
            jnp.concatenate([b_re * cos - b_im * sin, b_re * sin + b_im * cos], axis=0).astype(BF16)
        )
    result = dot(tables[768:832], jnp.concatenate(turned, axis=1))
    for c in range(8):
        piece = result[:, c * POINTS : (c + 1) * POINTS]
        out[pl.ds(c, 64, stride=8), :] = piece + skip[c] * rows[pl.ds(c, 64, stride=8), :]
    mixed[...] = out[...].astype(BF16).reshape(64, 8, POINTS)


def order_table(rows_are_natural, mine=0):
    shape = (512, 512)
    row = lax.broadcasted_iota(jnp.int32, shape, 0)
    col = lax.broadcasted_iota(jnp.int32, shape, 1)
    grouped, natural = (col, row) if rows_are_natural else (row, col)
    quarter, xy, j = (grouped // 128) ^ mine, (grouped // 8) % 16, grouped % 8
    place = (quarter // 2) * 256 + xy * 16 + (quarter % 2) * 8 + j
    return (natural == place).astype(F32).astype(BF16)


def weights_kernel(w_key, w_value, w_query, out):
    table = order_table(True)
    for p, ref in enumerate((w_key, w_value, w_query)):
        sorted_cols = dot(ref[...], table).astype(BF16)
        for quarter in range(4):
            piece = sorted_cols[:, quarter * 128 : (quarter + 1) * 128]
            for yh in range(4):
                out[quarter // 2, yh, quarter % 2, :, p * 128 : (p + 1) * 128] = piece


NEAR = (0, 1, -1, 2, -2)
FAR = (3, -3, 4)


def projected(where, near, far, near_other, far_other, w, at, width, acc):
    z, core = where[0], where[1]
    acc[...] = jnp.zeros_like(acc)
    for refs, steps in (((near, near_other), NEAR), ((far, far_other), FAR)):
        for i, step in enumerate(steps):
            source = (z + step) & 7
            rows_at = pl.ds(pl.multiple_of((source >> 2) * 2 * ROWS, 2 * ROWS), 2 * ROWS)
            total = acc[rows_at, :]
            for ref, half in zip(refs, (core, 1 - core)):
                part = (source & 3) * 2 + half
                weights = w[part & 3, part >> 2, :, :, at : at + width].reshape(512, width)
                total += dot(ref[i], weights)
            acc[rows_at, :] = total


def short(acc, group, at, taps):
    top = group * ROWS + HALO
    cols = pl.ds(at, 128)
    return (
        taps[0:1] * acc[pl.ds(top, BLOCK), cols]
        + taps[1:2] * acc[pl.ds(top - 1, BLOCK), cols]
        + taps[2:3] * acc[pl.ds(top - 2, BLOCK), cols]
    )


def key_value_kernel(where, near, far, near_other, far_other, w, taps, out, acc):
    projected(where, near, far, near_other, far_other, w, 0, 256, acc)
    for group in range(4):
        keyed = short(acc, group, 0, taps[1])
        valued = short(acc, group, 128, taps[2])
        out[:, group] = (keyed * valued).T.reshape(16, 8, BLOCK).astype(BF16)


def query_kernel(where, near, far, near_other, far_other, w, taps, out, acc):
    projected(where, near, far, near_other, far_other, w, 256, 128, acc)
    for group in range(4):
        out[group ^ where[2]] = short(acc, group, 0, taps[0]).astype(BF16)


def gate_kernel(where, q0, q1, q2, q3, returned, out):
    cols = jnp.concatenate([q0[0], q1[...], q2[...], q3[...]], axis=1)
    natural = dot(cols, order_table(False, where[2]))
    mixed = returned[...].astype(F32).reshape(512, BLOCK).T
    out[...] = (natural * mixed).astype(BF16)


def call(kernel, shape, dtype, args, scratch=(), in_specs=None, flops=10**8, name=None):
    whole = pl.BlockSpec(memory_space=pltpu.VMEM)
    specs = in_specs or [whole] * len(args)
    moved = sum(math.prod(a.shape) * a.dtype.itemsize for a in args)
    return pl.pallas_call(
        kernel,
        out_shape=jax.ShapeDtypeStruct(shape, dtype),
        in_specs=specs,
        out_specs=whole,
        scratch_shapes=list(scratch),
        compiler_params=pltpu.CompilerParams(vmem_limit_bytes=48 * 2**20),
        cost_estimate=pl.CostEstimate(flops=flops, bytes_accessed=moved, transcendentals=0),
        name=name,
    )(*args)


def shifted(value, axes, step, wrap=True):
    count = math.prod(SIZES[AXES.index(a)] for a in axes)
    pairs = [(i + step, i) for i in range(count) if wrap or 0 <= i + step < count]
    return lax.ppermute(value, axes, [(source % count, i) for source, i in pairs])


def swapped(value, axes, bits):
    count = math.prod(SIZES[AXES.index(a)] for a in axes)
    return lax.ppermute(value, axes, [(i, i ^ bits) for i in range(count)])


def local(tokens, w_query, w_key, w_value, short_taps, filters, skip_gain):
    place = lax.axis_index(AXES)
    core, z_lo, yl, z_hi = place % 2, place // 2 % 4, place // 8 % 2, place // 256
    where = jnp.stack([z_hi * 4 + z_lo, core, z_hi * 2 + yl])

    sent = call(weights_kernel, (2, 4, 2, 64, 384), BF16, (w_key, w_value, w_query), name="sort_weights")
    first = exchanged(sent.reshape(16, 64, 384), ("z_hi", "yh", "yl"))
    weights = from_everyone(first, ("x",)).reshape(4, 2, 8, 64, 384)

    halo = shifted(tokens[-HALO:], TOK, -1, wrap=False)
    mine = jnp.concatenate([halo, tokens], axis=0)
    other = swapped(mine, ("yl",), 1)
    first_half = yl == 0
    pair = jnp.concatenate(
        [jnp.where(first_half, mine, other), jnp.where(first_half, other, mine)], axis=0
    )
    ring = ("z_hi", "z_lo")
    ahead, behind = shifted(pair, ring, 2), shifted(pair, ring, -2)
    near = jnp.stack([pair, shifted(pair, ring, 1), shifted(pair, ring, -1), ahead, behind])
    near_other = swapped(near, ("core",), 1)
    far = jnp.stack([shifted(ahead, ring, 1), shifted(behind, ring, -1), shifted(ahead, ring, 2)])
    far_other = swapped(far, ("core",), 1)

    taps = short_taps.reshape(3, 3, 2, 16, 2, 8)
    taps = lax.dynamic_index_in_dim(taps, z_hi, 2, keepdims=False)
    taps = lax.dynamic_index_in_dim(taps, yl, 3, keepdims=False).reshape(3, 3, 128)

    tables, turns = dft_tables()
    spec = call(
        filter_kernel,
        (8 * POINTS, 2 * POINTS),
        F32,
        (filters, tables, turns),
        (pltpu.VMEM((512, POINTS), F32),),
        name="filter_spectrum",
    )

    whole = pl.BlockSpec(memory_space=pltpu.VMEM)
    smem = pl.BlockSpec(memory_space=pltpu.SMEM)
    features = (where, near, far, near_other, far_other, weights, taps)
    key_value = call(
        key_value_kernel,
        (16, 4, 8, BLOCK),
        BF16,
        features,
        (pltpu.VMEM((4 * ROWS, 256), F32),),
        in_specs=[smem] + [whole] * 6,
        flops=2 * 544 * 4096 * 256,
        name="key_value",
    )
    owned = exchanged(key_value, ("x", "yh"))
    query = call(
        query_kernel,
        (4, BLOCK, 128),
        BF16,
        features,
        (pltpu.VMEM((4 * ROWS, 128), F32),),
        in_specs=[smem] + [whole] * 6,
        flops=2 * 544 * 4096 * 128,
        name="query",
    )
    queries = [query] + [swapped(query[bits], ("z_hi", "yl"), bits) for bits in (1, 2, 3)]
    mixed = call(
        conv_kernel,
        (64, 8, BLOCK),
        BF16,
        (owned.reshape(16, 2, 2, 8, BLOCK), spec, skip_gain, tables, turns),
        (pltpu.VMEM((512, POINTS), F32), pltpu.VMEM((512, POINTS), F32)),
        in_specs=[whole, whole, smem, whole, whole],
        flops=2 * 168 * 10**6,
        name="long_conv",
    )
    returned = exchanged(mixed, TOK)
    return call(
        gate_kernel,
        (BLOCK, 512),
        BF16,
        (where, *queries, returned),
        in_specs=[smem] + [whole] * 5,
        name="gate",
    )


def solution(mesh):
    fine = Mesh(mesh.devices.reshape(SIZES), AXES)
    in_specs = (
        P(TOK, TP),
        P(TOK, TP),
        P(TOK, TP),
        P(TOK, TP),
        P(None, None, TP),
        P(TP + TOK, None),
        P(TP + TOK),
    )
    return jax.shard_map(local, mesh=fine, in_specs=in_specs, out_specs=P(TOK, TP), check_vma=False)
```

```python
import math

import jax
import jax.numpy as jnp
import numpy as np
from jax import lax
from jax.experimental import pallas as pl
from jax.experimental.pallas import tpu as pltpu
from jax.sharding import Mesh
from jax.sharding import PartitionSpec as P

AXES = ("z_hi", "x", "yh", "yl", "z_lo", "core")
SIZES = (2, 4, 4, 2, 4, 2)
TOK = AXES[:4]
TP = AXES[4:]
HALO = 8
BLOCK = 128
ROWS = HALO + BLOCK
POINTS = 128
F32 = jnp.float32
BF16 = jnp.bfloat16


def exchanged(value, axes):
    return lax.all_to_all(value, axes, split_axis=0, concat_axis=0, tiled=True)


def from_everyone(value, axes):
    count = math.prod(SIZES[AXES.index(a)] for a in axes)
    return exchanged(jnp.broadcast_to(value, (count, *value.shape)), axes)


def dft_tables():
    n = np.arange(POINTS)
    full = 2.0 * np.pi * (np.outer(n, n) % POINTS) / POINTS
    cos, sin = np.cos(full), np.sin(full)
    half = POINTS // 2
    outer = np.concatenate([cos, -sin], axis=0)
    outer = np.concatenate([outer, outer], axis=1)
    inner = np.block([[cos, -sin], [sin, cos]])
    back_inner = np.block([[cos, sin], [-sin, cos]])
    back_outer = np.concatenate([cos[:half], -sin[:half]], axis=1) / POINTS**2
    twist = 2.0 * np.pi * np.outer(n, n) / POINTS**2
    tables = np.concatenate([inner, back_inner, outer, back_outer], axis=0)
    turns = np.concatenate([np.cos(twist), np.sin(twist)], axis=0)
    return jnp.asarray(tables, F32).astype(BF16), jnp.asarray(turns, F32)


def dot(a, b):
    return jnp.dot(a, b, preferred_element_type=F32)


def spectrum(rows, tables, turns):
    cos, sin = turns[0:POINTS], turns[POINTS:]
    blocks = jnp.concatenate(
        [rows[pl.ds(c, 64, stride=8), :].astype(BF16) for c in range(8)], axis=1
    )
    first = dot(tables[512:768, 0:64], blocks)
    turned = []
    for c in range(8):
        re = first[:POINTS, c * POINTS : (c + 1) * POINTS]
        im = first[POINTS:, c * POINTS : (c + 1) * POINTS]
        turned.append(
            jnp.concatenate([re * cos + im * sin, im * cos - re * sin], axis=1).astype(BF16)
        )
    return dot(jnp.concatenate(turned, axis=0), tables[0:256])


def filter_kernel(filters, tables, turns, spec, rows):
    taps = filters[...]
    unit = taps / jnp.sqrt(jnp.sum(taps * taps, axis=1, keepdims=True) + 1e-06)
    for b in range(64):
        rows[pl.ds(b * 8, 8), :] = unit[:, b * POINTS : (b + 1) * POINTS]
    spec[...] = spectrum(rows, tables, turns)


def conv_kernel(signal, spec, skip, tables, turns, mixed, rows, out):
    for z in range(2):
        rows[pl.ds(z * 256, 256), :] = signal[:, z].astype(F32).reshape(256, POINTS)
    cos, sin = turns[0:POINTS], turns[POINTS:]
    sig = spectrum(rows, tables, turns)
    re, im = sig[:, :POINTS], sig[:, POINTS:]
    f_re, f_im = spec[:, :POINTS], spec[:, POINTS:]
    prod = jnp.concatenate([re * f_re - im * f_im, re * f_im + im * f_re], axis=1)
    back = dot(prod.astype(BF16), tables[256:512])
    turned = []
    for c in range(8):
        b_re = back[c * POINTS : (c + 1) * POINTS, :POINTS]
        b_im = back[c * POINTS : (c + 1) * POINTS, POINTS:]
        turned.append(
            jnp.concatenate([b_re * cos - b_im * sin, b_re * sin + b_im * cos], axis=0).astype(BF16)
        )
    result = dot(tables[768:832], jnp.concatenate(turned, axis=1))
    for c in range(8):
        piece = result[:, c * POINTS : (c + 1) * POINTS]
        out[pl.ds(c, 64, stride=8), :] = piece + skip[c] * rows[pl.ds(c, 64, stride=8), :]
    mixed[...] = out[...].astype(BF16).reshape(64, 8, POINTS)


def order_table(rows_are_natural, mine=0):
    shape = (512, 512)
    row = lax.broadcasted_iota(jnp.int32, shape, 0)
    col = lax.broadcasted_iota(jnp.int32, shape, 1)
    grouped, natural = (col, row) if rows_are_natural else (row, col)
    quarter, xy, j = (grouped // 128) ^ mine, (grouped // 8) % 16, grouped % 8
    place = (quarter // 2) * 256 + xy * 16 + (quarter % 2) * 8 + j
    return (natural == place).astype(F32).astype(BF16)


def weights_kernel(w_key, w_value, w_query, out):
    table = order_table(True)
    for p, ref in enumerate((w_key, w_value, w_query)):
        sorted_cols = dot(ref[...], table).astype(BF16)
        for quarter in range(4):
            piece = sorted_cols[:, quarter * 128 : (quarter + 1) * 128]
            for yh in range(4):
                out[quarter // 2, yh, quarter % 2, :, p * 128 : (p + 1) * 128] = piece


NEAR = (0, 1, -1, 2, -2)
FAR = (3, -3, 4)


def projected(where, near, far, near_other, far_other, w, at, width, acc):
    z, core = where[0], where[1]
    acc[...] = jnp.zeros_like(acc)
    for refs, steps in (((near, near_other), NEAR), ((far, far_other), FAR)):
        for i, step in enumerate(steps):
            source = (z + step) & 7
            rows_at = pl.ds(pl.multiple_of((source >> 2) * 2 * ROWS, 2 * ROWS), 2 * ROWS)
            total = acc[rows_at, :]
            for ref, half in zip(refs, (core, 1 - core)):
                part = (source & 3) * 2 + half
                weights = w[part & 3, part >> 2, :, :, at : at + width].reshape(512, width)
                total += dot(ref[i], weights)
            acc[rows_at, :] = total


def short(acc, group, at, taps):
    top = group * ROWS + HALO
    cols = pl.ds(at, 128)
    return (
        taps[0:1] * acc[pl.ds(top, BLOCK), cols]
        + taps[1:2] * acc[pl.ds(top - 1, BLOCK), cols]
        + taps[2:3] * acc[pl.ds(top - 2, BLOCK), cols]
    )


def key_value_kernel(where, near, far, near_other, far_other, w, taps, out, acc):
    projected(where, near, far, near_other, far_other, w, 0, 256, acc)
    for group in range(4):
        keyed = short(acc, group, 0, taps[1])
        valued = short(acc, group, 128, taps[2])
        out[:, group] = (keyed * valued).T.reshape(16, 8, BLOCK).astype(BF16)


def query_kernel(where, near, far, near_other, far_other, w, taps, out, acc):
    projected(where, near, far, near_other, far_other, w, 256, 128, acc)
    for group in range(4):
        out[group ^ where[2]] = short(acc, group, 0, taps[0]).astype(BF16)


def gate_kernel(where, q0, q1, q2, q3, returned, out):
    cols = jnp.concatenate([q0[0], q1[...], q2[...], q3[...]], axis=1)
    natural = dot(cols, order_table(False, where[2]))
    mixed = returned[...].astype(F32).reshape(512, BLOCK).T
    out[...] = (natural * mixed).astype(BF16)


def call(kernel, shape, dtype, args, scratch=(), in_specs=None, flops=10**8, name=None):
    whole = pl.BlockSpec(memory_space=pltpu.VMEM)
    specs = in_specs or [whole] * len(args)
    moved = sum(math.prod(a.shape) * a.dtype.itemsize for a in args)
    return pl.pallas_call(
        kernel,
        out_shape=jax.ShapeDtypeStruct(shape, dtype),
        in_specs=specs,
        out_specs=whole,
        scratch_shapes=list(scratch),
        compiler_params=pltpu.CompilerParams(vmem_limit_bytes=20 * 2**20),
        cost_estimate=pl.CostEstimate(flops=flops, bytes_accessed=moved, transcendentals=0),
        name=name,
    )(*args)


def shifted(value, axes, step, wrap=True):
    count = math.prod(SIZES[AXES.index(a)] for a in axes)
    pairs = [(i + step, i) for i in range(count) if wrap or 0 <= i + step < count]
    return lax.ppermute(value, axes, [(source % count, i) for source, i in pairs])


def swapped(value, axes, bits):
    count = math.prod(SIZES[AXES.index(a)] for a in axes)
    return lax.ppermute(value, axes, [(i, i ^ bits) for i in range(count)])


def both_halves(blocks, yl):
    other = swapped(blocks, ("yl",), 1)
    first = yl == 0
    halves = [jnp.where(first, blocks, other), jnp.where(first, other, blocks)]
    return jnp.concatenate(halves, axis=1)


def local(tokens, w_query, w_key, w_value, short_taps, filters, skip_gain):
    place = lax.axis_index(AXES)
    core, z_lo, yl, z_hi = place % 2, place // 2 % 4, place // 8 % 2, place // 256
    where = jnp.stack([z_hi * 4 + z_lo, core, z_hi * 2 + yl])

    sent = call(weights_kernel, (2, 4, 2, 64, 384), BF16, (w_key, w_value, w_query), name="sort_weights")
    first = exchanged(sent.reshape(16, 64, 384), ("z_hi", "yh", "yl"))

    halo = shifted(tokens[-HALO:], TOK, -1, wrap=False)
    mine = jnp.concatenate([halo, tokens], axis=0)
    ring = ("z_hi", "z_lo")
    ahead, behind = shifted(mine, ring, 2), shifted(mine, ring, -2)
    near = both_halves(jnp.stack([mine, shifted(mine, ring, 1), shifted(mine, ring, -1), ahead, behind]), yl)
    near_other = swapped(near, ("core",), 1)
    far = both_halves(
        jnp.stack([shifted(ahead, ring, 1), shifted(behind, ring, -1), shifted(ahead, ring, 2)]), yl
    )
    far_other = swapped(far, ("core",), 1)

    taps = short_taps.reshape(3, 3, 2, 16, 2, 8)
    taps = lax.dynamic_index_in_dim(taps, z_hi, 2, keepdims=False)
    taps = lax.dynamic_index_in_dim(taps, yl, 3, keepdims=False).reshape(3, 3, 128)

    tables, turns = dft_tables()
    spec = call(
        filter_kernel,
        (8 * POINTS, 2 * POINTS),
        F32,
        (filters, tables, turns),
        (pltpu.VMEM((512, POINTS), F32),),
        name="filter_spectrum",
    )

    first, spec, taps = lax.optimization_barrier((first, spec, taps))
    weights = from_everyone(first, ("x",)).reshape(4, 2, 8, 64, 384)

    whole = pl.BlockSpec(memory_space=pltpu.VMEM)
    smem = pl.BlockSpec(memory_space=pltpu.SMEM)
    features = (where, near, far, near_other, far_other, weights, taps)
    key_value = call(
        key_value_kernel,
        (16, 4, 8, BLOCK),
        BF16,
        features,
        (pltpu.VMEM((4 * ROWS, 256), F32),),
        in_specs=[smem] + [whole] * 6,
        flops=2 * 544 * 4096 * 256,
        name="key_value",
    )
    owned = exchanged(key_value, ("x", "yh"))
    query = call(
        query_kernel,
        (4, BLOCK, 128),
        BF16,
        features,
        (pltpu.VMEM((4 * ROWS, 128), F32),),
        in_specs=[smem] + [whole] * 6,
        flops=2 * 544 * 4096 * 128,
        name="query",
    )
    queries = [query] + [swapped(query[bits], ("z_hi", "yl"), bits) for bits in (1, 2, 3)]
    owned, *queries = lax.optimization_barrier((owned, *queries))
    mixed = call(
        conv_kernel,
        (64, 8, BLOCK),
        BF16,
        (owned.reshape(16, 2, 2, 8, BLOCK), spec, skip_gain, tables, turns),
        (pltpu.VMEM((512, POINTS), F32), pltpu.VMEM((512, POINTS), F32)),
        in_specs=[whole, whole, smem, whole, whole],
        flops=2 * 168 * 10**6,
        name="long_conv",
    )
    returned = exchanged(mixed, TOK)
    return call(
        gate_kernel,
        (BLOCK, 512),
        BF16,
        (where, *queries, returned),
        in_specs=[smem] + [whole] * 5,
        name="gate",
    )


def solution(mesh):
    fine = Mesh(mesh.devices.reshape(SIZES), AXES)
    in_specs = (
        P(TOK, TP),
        P(TOK, TP),
        P(TOK, TP),
        P(TOK, TP),
        P(None, None, TP),
        P(TP + TOK, None),
        P(TP + TOK),
    )
    return jax.shard_map(local, mesh=fine, in_specs=in_specs, out_specs=P(TOK, TP), check_vma=False)
```

```python
import math

import jax
import jax.numpy as jnp
import numpy as np
from jax import lax
from jax.experimental import pallas as pl
from jax.experimental.pallas import tpu as pltpu
from jax.sharding import Mesh
from jax.sharding import PartitionSpec as P

AXES = ("z_hi", "x", "yh", "yl", "z_lo", "core")
SIZES = (2, 4, 4, 2, 4, 2)
TOK = AXES[:4]
TP = AXES[4:]
HALO = 8
BLOCK = 128
ROWS = HALO + BLOCK
POINTS = 128
F32 = jnp.float32
BF16 = jnp.bfloat16


def exchanged(value, axes):
    return lax.all_to_all(value, axes, split_axis=0, concat_axis=0, tiled=True)


def from_everyone(value, axes):
    count = math.prod(SIZES[AXES.index(a)] for a in axes)
    return exchanged(jnp.broadcast_to(value, (count, *value.shape)), axes)


def dft_tables():
    n = np.arange(POINTS)
    full = 2.0 * np.pi * (np.outer(n, n) % POINTS) / POINTS
    cos, sin = np.cos(full), np.sin(full)
    half = POINTS // 2
    outer = np.concatenate([cos, -sin], axis=0)
    outer = np.concatenate([outer, outer], axis=1)
    inner = np.block([[cos, -sin], [sin, cos]])
    back_inner = np.block([[cos, sin], [-sin, cos]])
    back_outer = np.concatenate([cos[:half], -sin[:half]], axis=1) / POINTS**2
    twist = 2.0 * np.pi * np.outer(n, n) / POINTS**2
    tables = np.concatenate([inner, back_inner, outer, back_outer], axis=0)
    turns = np.concatenate([np.cos(twist), np.sin(twist)], axis=0)
    return jnp.asarray(tables, F32).astype(BF16), jnp.asarray(turns, F32)


def dot(a, b):
    return jnp.dot(a, b, preferred_element_type=F32)


def spectrum(rows, tables, turns):
    cos, sin = turns[0:POINTS], turns[POINTS:]
    blocks = jnp.concatenate(
        [rows[pl.ds(c, 64, stride=8), :].astype(BF16) for c in range(8)], axis=1
    )
    first = dot(tables[512:768, 0:64], blocks)
    turned = []
    for c in range(8):
        re = first[:POINTS, c * POINTS : (c + 1) * POINTS]
        im = first[POINTS:, c * POINTS : (c + 1) * POINTS]
        turned.append(
            jnp.concatenate([re * cos + im * sin, im * cos - re * sin], axis=1).astype(BF16)
        )
    return dot(jnp.concatenate(turned, axis=0), tables[0:256])


def filter_kernel(filters, tables, turns, spec, tables_out, turns_out, rows):
    tables_out[...] = tables[...]
    turns_out[...] = turns[...]
    taps = filters[...]
    unit = taps / jnp.sqrt(jnp.sum(taps * taps, axis=1, keepdims=True) + 1e-06)
    for b in range(64):
        rows[pl.ds(b * 8, 8), :] = unit[:, b * POINTS : (b + 1) * POINTS]
    spec[...] = spectrum(rows, tables, turns)


def conv_kernel(signal, spec, skip, tables, turns, mixed, rows, out):
    for z in range(2):
        rows[pl.ds(z * 256, 256), :] = signal[:, z].astype(F32).reshape(256, POINTS)
    cos, sin = turns[0:POINTS], turns[POINTS:]
    sig = spectrum(rows, tables, turns)
    re, im = sig[:, :POINTS], sig[:, POINTS:]
    f_re, f_im = spec[:, :POINTS], spec[:, POINTS:]
    prod = jnp.concatenate([re * f_re - im * f_im, re * f_im + im * f_re], axis=1)
    back = dot(prod.astype(BF16), tables[256:512])
    turned = []
    for c in range(8):
        b_re = back[c * POINTS : (c + 1) * POINTS, :POINTS]
        b_im = back[c * POINTS : (c + 1) * POINTS, POINTS:]
        turned.append(
            jnp.concatenate([b_re * cos - b_im * sin, b_re * sin + b_im * cos], axis=0).astype(BF16)
        )
    result = dot(tables[768:832], jnp.concatenate(turned, axis=1))
    for c in range(8):
        piece = result[:, c * POINTS : (c + 1) * POINTS]
        out[pl.ds(c, 64, stride=8), :] = piece + skip[c] * rows[pl.ds(c, 64, stride=8), :]
    mixed[...] = out[...].astype(BF16).reshape(64, 8, POINTS)


def order_table(rows_are_natural, mine=0):
    shape = (512, 512)
    row = lax.broadcasted_iota(jnp.int32, shape, 0)
    col = lax.broadcasted_iota(jnp.int32, shape, 1)
    grouped, natural = (col, row) if rows_are_natural else (row, col)
    quarter, xy, j = (grouped // 128) ^ mine, (grouped // 8) % 16, grouped % 8
    place = (quarter // 2) * 256 + xy * 16 + (quarter % 2) * 8 + j
    return (natural == place).astype(F32).astype(BF16)


def weights_kernel(w_key, w_value, w_query, out):
    table = order_table(True)
    for p, ref in enumerate((w_key, w_value, w_query)):
        sorted_cols = dot(ref[...], table).astype(BF16)
        for quarter in range(4):
            piece = sorted_cols[:, quarter * 128 : (quarter + 1) * 128]
            for yh in range(4):
                out[quarter // 2, yh, quarter % 2, p] = piece


def fetched(sources, held, sems):
    copies = [pltpu.make_async_copy(a, b, sems.at[i]) for i, (a, b) in enumerate(zip(sources, held))]
    for copy in copies:
        copy.start()
    return copies


def projected(where, features, w, acc, ready):
    z, core = where[0], where[1]
    for i, (half, low) in enumerate((h, l) for h in range(2) for l in (0, 2, 1, 3)):
        if i % 2 == 0:
            for parity in range(2):
                ready[half * 4 + parity * 2 + low % 2].wait()
        part = ((z ^ low) & 3) * 2 + (core ^ half)
        pieces = [
            features[half * 4 + parity * 2 + low % 2][(low // 2) * 2 : (low // 2) * 2 + 2]
            for parity in range(2)
        ]
        rows = jnp.concatenate([p.reshape(2 * ROWS, 512) for p in pieces], axis=0)
        term = dot(rows, w(part))
        if i == 0:
            acc[...] = term
        else:
            acc[...] += term


def group_of(where, i):
    return ((i % 2) * 2 + i // 2) ^ where[2]


def short(acc, group, at, taps):
    top = group * ROWS + HALO
    cols = pl.ds(at, 128)
    return (
        taps[0:1] * acc[pl.ds(top, BLOCK), cols]
        + taps[1:2] * acc[pl.ds(top - 1, BLOCK), cols]
        + taps[2:3] * acc[pl.ds(top - 2, BLOCK), cols]
    )


def key_value_kernel(where, *refs):
    sources, (w, taps, out), held, (acc, sems) = refs[:8], refs[8:11], refs[11:19], refs[19:]
    copies = fetched(sources, held, sems)

    def weights(part):
        block = w[part & 3, part >> 2]
        return jnp.concatenate([block[:, p].reshape(512, 128) for p in range(2)], axis=1)

    projected(where, held, weights, acc, copies)
    for i in range(4):
        keyed = short(acc, i, 0, taps[1])
        valued = short(acc, i, 128, taps[2])
        out[:, group_of(where, i)] = (keyed * valued).T.reshape(16, 8, BLOCK).astype(BF16)


def query_kernel(where, *refs):
    sources, (taps, out), held, (w, acc, sems) = refs[:12], refs[12:14], refs[14:22], refs[22:]
    targets = [w.at[d] for d in range(4)] + list(held)
    copies = fetched(sources[8:] + sources[:8], targets, sems)
    for copy in copies[:4]:
        copy.wait()

    def weights(part):
        return w[(part & 3) ^ where[3], part >> 2].reshape(512, 128)

    projected(where, held, weights, acc, copies[4:])
    for i in range(4):
        out[(i % 2) * 2 + i // 2] = short(acc, i, 0, taps[0]).astype(BF16)


def gate_kernel(where, q0, q1, q2, q3, returned, out):
    cols = jnp.concatenate([q0[0], q1[...], q2[...], q3[...]], axis=1)
    natural = dot(cols, order_table(False, where[2]))
    mixed = returned[...].astype(F32).reshape(512, BLOCK).T
    out[...] = (natural * mixed).astype(BF16)


def call(kernel, out_shape, args, scratch=(), in_specs=None, flops=10**8, name=None):
    whole = pl.BlockSpec(memory_space=pltpu.VMEM)
    specs = in_specs or [whole] * len(args)
    moved = sum(math.prod(a.shape) * a.dtype.itemsize for a in args)
    return pl.pallas_call(
        kernel,
        out_shape=out_shape,
        in_specs=specs,
        out_specs=jax.tree.map(lambda _: whole, out_shape),
        scratch_shapes=list(scratch),
        compiler_params=pltpu.CompilerParams(vmem_limit_bytes=20 * 2**20),
        cost_estimate=pl.CostEstimate(flops=flops, bytes_accessed=moved, transcendentals=0),
        name=name,
    )(*args)


def of_previous(value, axes):
    count = math.prod(SIZES[AXES.index(a)] for a in axes)
    return lax.ppermute(value, axes, [(i, i + 1) for i in range(count - 1)])


def swapped(value, axes, bits):
    count = math.prod(SIZES[AXES.index(a)] for a in axes)
    return lax.ppermute(value, axes, [(i, i ^ bits) for i in range(count)])


def local(tokens, w_query, w_key, w_value, short_taps, filters, skip_gain):
    shape = jax.ShapeDtypeStruct
    whole = pl.BlockSpec(memory_space=pltpu.VMEM)
    smem = pl.BlockSpec(memory_space=pltpu.SMEM)
    place = lax.axis_index(AXES)
    core, z_lo, yl, x, z_hi = place % 2, place // 2 % 4, place // 8 % 2, place // 64 % 4, place // 256
    where = jnp.stack([z_hi * 4 + z_lo, core, z_hi * 2 + yl, x])

    halo = of_previous(tokens[-HALO:], TOK)
    sent = call(
        weights_kernel, shape((2, 4, 2, 3, 64, 128), BF16), (w_key, w_value, w_query), name="sort_weights"
    )
    sent, halo = lax.optimization_barrier((sent, halo))
    first = exchanged(sent.reshape(16, 3, 64, 128), ("z_hi", "yh", "yl"))

    ring = ("z_hi", "z_lo")
    mine = jnp.concatenate([halo, tokens], axis=0)[None]
    two = jnp.concatenate([mine, swapped(mine, ring, 4)], axis=0)
    even = jnp.concatenate([two, swapped(two, ring, 2)], axis=0)
    odd = swapped(even, ring, 1)
    even_y = swapped(even, ("yl",), 1)
    odd_y = swapped(odd, ("yl",), 1)
    ours = (even, odd, even_y, odd_y)
    features = ours + tuple(swapped(v, ("core",), 1) for v in ours)

    taps = short_taps.reshape(3, 3, 2, 16, 2, 8)
    taps = lax.dynamic_index_in_dim(taps, z_hi, 2, keepdims=False)
    taps = lax.dynamic_index_in_dim(taps, yl, 3, keepdims=False).reshape(3, 3, 128)

    first, taps, where = lax.optimization_barrier((first, taps, where))
    weights = from_everyone(first[:, :2], ("x",)).reshape(4, 2, 8, 2, 64, 128)
    first_query, _ = lax.optimization_barrier((first[:, 2], odd_y))
    first_query = first_query.reshape(2, 8, 64, 128)
    query_weights = [first_query] + [swapped(first_query, ("x",), d) for d in (1, 2, 3)]

    anywhere = pl.BlockSpec(memory_space=pl.ANY)
    kept = [pltpu.with_memory_space_constraint(v, pltpu.HBM) for v in features]
    blocks = [pltpu.VMEM((4, ROWS, 512), BF16)] * 8
    key_value = call(
        key_value_kernel,
        shape((16, 4, 8, BLOCK), BF16),
        (where, *kept, weights, taps),
        blocks + [pltpu.VMEM((4 * ROWS, 256), F32), pltpu.SemaphoreType.DMA((8,))],
        in_specs=[smem] + [anywhere] * 8 + [whole] * 2,
        flops=2 * 544 * 4096 * 256,
        name="key_value",
    )
    key_value, query_weights[0] = lax.optimization_barrier((key_value, query_weights[0]))
    owned = exchanged(key_value, ("x", "yh"))
    query = call(
        query_kernel,
        shape((4, BLOCK, 128), BF16),
        (where, *kept, *query_weights, taps),
        blocks
        + [
            pltpu.VMEM((4, 2, 8, 64, 128), BF16),
            pltpu.VMEM((4 * ROWS, 128), F32),
            pltpu.SemaphoreType.DMA((12,)),
        ],
        in_specs=[smem] + [anywhere] * 12 + [whole],
        flops=2 * 544 * 4096 * 128,
        name="query",
    )
    tables, turns = dft_tables()
    filters, _ = lax.optimization_barrier((filters, key_value))
    spec, tables, turns = call(
        filter_kernel,
        (shape((8 * POINTS, 2 * POINTS), F32), shape(tables.shape, BF16), shape(turns.shape, F32)),
        (filters, tables, turns),
        (pltpu.VMEM((512, POINTS), F32),),
        name="filter_spectrum",
    )
    queries = [query] + [swapped(query[bits], ("z_hi", "yl"), bits) for bits in (1, 2, 3)]
    owned, queries[1], spec = lax.optimization_barrier((owned, queries[1], spec))
    mixed = call(
        conv_kernel,
        shape((64, 8, BLOCK), BF16),
        (owned.reshape(16, 2, 2, 8, BLOCK), spec, skip_gain, tables, turns),
        (pltpu.VMEM((512, POINTS), F32), pltpu.VMEM((512, POINTS), F32)),
        in_specs=[whole, whole, smem, whole, whole],
        flops=2 * 168 * 10**6,
        name="long_conv",
    )
    returned = exchanged(mixed, TOK)
    return call(
        gate_kernel,
        shape((BLOCK, 512), BF16),
        (where, *queries, returned),
        in_specs=[smem] + [whole] * 5,
        name="gate",
    )


def solution(mesh):
    fine = Mesh(mesh.devices.reshape(SIZES), AXES)
    in_specs = (
        P(TOK, TP),
        P(TOK, TP),
        P(TOK, TP),
        P(TOK, TP),
        P(None, None, TP),
        P(TP + TOK, None),
        P(TP + TOK),
    )
    return jax.shard_map(local, mesh=fine, in_specs=in_specs, out_specs=P(TOK, TP), check_vma=False)
```

```python
import math

import jax
import jax.numpy as jnp
import numpy as np
from jax import lax
from jax.experimental import pallas as pl
from jax.experimental.pallas import tpu as pltpu
from jax.sharding import Mesh
from jax.sharding import PartitionSpec as P

AXES = ("z_hi", "x", "yh", "yl", "z_lo", "core")
SIZES = (2, 4, 4, 2, 4, 2)
TOK = AXES[:4]
TP = AXES[4:]
HALO = 8
BLOCK = 128
ROWS = HALO + BLOCK
POINTS = 128
F32 = jnp.float32
BF16 = jnp.bfloat16


def exchanged(value, axes):
    return lax.all_to_all(value, axes, split_axis=0, concat_axis=0, tiled=True)


def from_everyone(value, axes, apart=()):
    count = math.prod(SIZES[AXES.index(a)] for a in axes)
    copies = jnp.broadcast_to(value, (count, *value.shape))
    if apart:
        copies = copies.reshape(-1, *value.shape[1:])
    return exchanged(copies, axes + apart)


def dft_tables():
    n = np.arange(POINTS)
    full = 2.0 * np.pi * (np.outer(n, n) % POINTS) / POINTS
    cos, sin = np.cos(full), np.sin(full)
    half = POINTS // 2
    outer = np.concatenate([cos, -sin], axis=0)
    outer = np.concatenate([outer, outer], axis=1)
    inner = np.block([[cos, -sin], [sin, cos]])
    back_inner = np.block([[cos, sin], [-sin, cos]])
    back_outer = np.concatenate([cos[:half], -sin[:half]], axis=1) / POINTS**2
    twist = 2.0 * np.pi * np.outer(n, n) / POINTS**2
    tables = np.concatenate([inner, back_inner, outer, back_outer], axis=0)
    turns = np.concatenate([np.cos(twist), np.sin(twist)], axis=0)
    return jnp.asarray(tables, F32).astype(BF16), jnp.asarray(turns, F32)


def dot(a, b):
    return jnp.dot(a, b, preferred_element_type=F32)


def spectrum(rows, tables, turns):
    cos, sin = turns[0:POINTS], turns[POINTS:]
    blocks = jnp.concatenate(
        [rows[pl.ds(c, 64, stride=8), :].astype(BF16) for c in range(8)], axis=1
    )
    first = dot(tables[512:768, 0:64], blocks)
    turned = []
    for c in range(8):
        re = first[:POINTS, c * POINTS : (c + 1) * POINTS]
        im = first[POINTS:, c * POINTS : (c + 1) * POINTS]
        turned.append(
            jnp.concatenate([re * cos + im * sin, im * cos - re * sin], axis=1).astype(BF16)
        )
    return dot(jnp.concatenate(turned, axis=0), tables[0:256])


def filter_kernel(filters, tables, turns, spec, tables_out, turns_out, rows):
    tables_out[...] = tables[...]
    turns_out[...] = turns[...]
    taps = filters[...]
    unit = taps / jnp.sqrt(jnp.sum(taps * taps, axis=1, keepdims=True) + 1e-06)
    for b in range(64):
        rows[pl.ds(b * 8, 8), :] = unit[:, b * POINTS : (b + 1) * POINTS]
    spec[...] = spectrum(rows, tables, turns)


def conv_kernel(signal, spec, skip, tables, turns, mixed, rows, out):
    for z in range(2):
        rows[pl.ds(z * 256, 256), :] = signal[:, z].astype(F32).reshape(256, POINTS)
    cos, sin = turns[0:POINTS], turns[POINTS:]
    sig = spectrum(rows, tables, turns)
    re, im = sig[:, :POINTS], sig[:, POINTS:]
    f_re, f_im = spec[:, :POINTS], spec[:, POINTS:]
    prod = jnp.concatenate([re * f_re - im * f_im, re * f_im + im * f_re], axis=1)
    back = dot(prod.astype(BF16), tables[256:512])
    turned = []
    for c in range(8):
        b_re = back[c * POINTS : (c + 1) * POINTS, :POINTS]
        b_im = back[c * POINTS : (c + 1) * POINTS, POINTS:]
        turned.append(
            jnp.concatenate([b_re * cos - b_im * sin, b_re * sin + b_im * cos], axis=0).astype(BF16)
        )
    result = dot(tables[768:832], jnp.concatenate(turned, axis=1))
    for c in range(8):
        piece = result[:, c * POINTS : (c + 1) * POINTS]
        out[pl.ds(c, 64, stride=8), :] = piece + skip[c] * rows[pl.ds(c, 64, stride=8), :]
    mixed[...] = out[...].astype(BF16).reshape(64, 8, POINTS)


def order_table(rows_are_natural, mine=0):
    shape = (512, 512)
    row = lax.broadcasted_iota(jnp.int32, shape, 0)
    col = lax.broadcasted_iota(jnp.int32, shape, 1)
    grouped, natural = (col, row) if rows_are_natural else (row, col)
    quarter, xy, j = (grouped // 128) ^ mine, (grouped // 8) % 16, grouped % 8
    place = (quarter // 2) * 256 + xy * 16 + (quarter % 2) * 8 + j
    return (natural == place).astype(F32).astype(BF16)


def weights_kernel(where, w_key, w_value, w_query, mine, theirs, held, sems):
    copies = fetched((w_key, w_value, w_query), [held.at[p] for p in range(3)], sems)
    table = order_table(True)
    lower = where[2] < 2
    for p in range(3):
        copies[p].wait()
        cols = dot(held[p], table)
        ours = jnp.where(lower, cols[:, :256], cols[:, 256:]).astype(BF16)
        others = jnp.where(lower, cols[:, 256:], cols[:, :256]).astype(BF16)
        for yl in range(2):
            mine[yl, p] = ours[:, yl * 128 : (yl + 1) * 128]
            theirs[yl, p] = others[:, yl * 128 : (yl + 1) * 128]


def fetched(sources, held, sems):
    copies = [pltpu.make_async_copy(a, b, sems.at[i]) for i, (a, b) in enumerate(zip(sources, held))]
    for copy in copies:
        copy.start()
    return copies


def projected(where, features, w, acc, ready):
    z, core = where[0], where[1]
    for i, (half, low) in enumerate((h, l) for h in range(2) for l in (0, 2, 1, 3)):
        if i % 2 == 0:
            for parity in range(2):
                ready[half * 4 + parity * 2 + low % 2].wait()
        part = ((z ^ low) & 3) * 2 + (core ^ half)
        pieces = [
            features[half * 4 + parity * 2 + low % 2][(low // 2) * 2 : (low // 2) * 2 + 2]
            for parity in range(2)
        ]
        rows = jnp.concatenate([p.reshape(2 * ROWS, 512) for p in pieces], axis=0)
        term = dot(rows, w(part))
        if i == 0:
            acc[...] = term
        else:
            acc[...] += term


def group_of(where, i):
    return ((i % 2) * 2 + i // 2) ^ where[2]


def short(acc, group, at, taps):
    top = group * ROWS + HALO
    cols = pl.ds(at, 128)
    return (
        taps[0:1] * acc[pl.ds(top, BLOCK), cols]
        + taps[1:2] * acc[pl.ds(top - 1, BLOCK), cols]
        + taps[2:3] * acc[pl.ds(top - 2, BLOCK), cols]
    )


def key_value_kernel(where, *refs):
    sources, (taps, out), (w, *held), (acc, sems) = refs[:9], refs[9:11], refs[11:20], refs[20:]
    copies = fetched((sources[0].at[:, :, :, 0:2], *sources[1:]), (w, *held), sems)
    copies[0].wait()

    def weights(part):
        block = w[part & 3, :, (part >> 2) ^ where[3]]
        return jnp.concatenate([block[:, p].reshape(512, 128) for p in range(2)], axis=1)

    projected(where, held, weights, acc, copies[1:])
    for i in range(4):
        keyed = short(acc, i, 0, taps[1])
        valued = short(acc, i, 128, taps[2])
        out[:, group_of(where, i)] = (keyed * valued).T.reshape(16, 8, BLOCK).astype(BF16)


def query_kernel(where, *refs):
    sources, (taps, out), (w, *held), (acc, sems) = refs[:9], refs[9:11], refs[11:20], refs[20:]
    copies = fetched((sources[0].at[:, :, :, 2], *sources[1:]), (w, *held), sems)
    copies[0].wait()

    def weights(part):
        return w[part & 3, :, (part >> 2) ^ where[3]].reshape(512, 128)

    projected(where, held, weights, acc, copies[1:])
    for i in range(4):
        out[i // 2, i % 2] = short(acc, i, 0, taps[0]).astype(BF16)


def gate_kernel(where, query, near, far, returned, out):
    cols = jnp.concatenate([query[0, 0], near[0], far[0], far[1]], axis=1)
    natural = dot(cols, order_table(False, where[2]))
    mixed = returned[...].astype(F32).reshape(512, BLOCK).T
    out[...] = (natural * mixed).astype(BF16)


def call(kernel, out_shape, args, scratch=(), in_specs=None, flops=10**8):
    whole = pl.BlockSpec(memory_space=pltpu.VMEM)
    specs = in_specs or [whole] * len(args)
    moved = sum(math.prod(a.shape) * a.dtype.itemsize for a in args)
    return pl.pallas_call(
        kernel,
        out_shape=out_shape,
        in_specs=specs,
        out_specs=jax.tree.map(lambda _: whole, out_shape),
        scratch_shapes=list(scratch),
        compiler_params=pltpu.CompilerParams(vmem_limit_bytes=20 * 2**20),
        cost_estimate=pl.CostEstimate(flops=flops, bytes_accessed=moved, transcendentals=0),
    )(*args)


def of_previous(value, axes):
    count = math.prod(SIZES[AXES.index(a)] for a in axes)
    return lax.ppermute(value, axes, [(i, i + 1) for i in range(count - 1)])


def swapped(value, axes, bits):
    count = math.prod(SIZES[AXES.index(a)] for a in axes)
    return lax.ppermute(value, axes, [(i, i ^ bits) for i in range(count)])


def mixer(tokens, w_query, w_key, w_value, short_taps, filters, skip_gain):
    shape = jax.ShapeDtypeStruct
    whole = pl.BlockSpec(memory_space=pltpu.VMEM)
    smem = pl.BlockSpec(memory_space=pltpu.SMEM)
    place = lax.axis_index(AXES)
    core, z_lo, yl, z_hi = place % 2, place // 2 % 4, place // 8 % 2, place // 256
    where = jnp.stack([z_hi * 4 + z_lo, core, z_hi * 2 + yl, z_hi])

    anywhere = pl.BlockSpec(memory_space=pl.ANY)
    halo = of_previous(tokens[-HALO:], TOK)
    part = shape((2, 3, 64, 128), BF16)
    own, others = call(
        weights_kernel,
        (part, part),
        (where, *(pltpu.with_memory_space_constraint(w, pltpu.HBM) for w in (w_key, w_value, w_query))),
        (pltpu.VMEM((3, 64, 512), BF16), pltpu.SemaphoreType.DMA((3,))),
        in_specs=[smem] + [anywhere] * 3,
    )
    others, halo = lax.optimization_barrier((others, halo))
    got = swapped(others, ("z_hi",), 1)
    first = from_everyone(jnp.stack([own, got], axis=1), ("yh",), ("yl",))

    ring = ("z_hi", "z_lo")
    mine = jnp.concatenate([halo, tokens], axis=0)[None]
    far_block = swapped(mine, ring, 4)
    two = jnp.concatenate([mine, far_block], axis=0)
    even = jnp.concatenate([two, swapped(two, ring, 2)], axis=0)
    taps = short_taps.reshape(3, 3, 2, 16, 2, 8)
    taps = lax.dynamic_index_in_dim(taps, z_hi, 2, keepdims=False)
    taps = lax.dynamic_index_in_dim(taps, yl, 3, keepdims=False).reshape(3, 3, 128)

    first, taps, where, _ = lax.optimization_barrier((first, taps, where, even))
    weights = from_everyone(first, ("x",))
    odd = swapped(even, ring, 1)
    even_y = swapped(even, ("yl",), 1)
    odd_y = swapped(odd, ("yl",), 1)
    ours = (even, odd, even_y, odd_y)
    features = ours + tuple(swapped(v, ("core",), 1) for v in ours)


    kept = [pltpu.with_memory_space_constraint(v, pltpu.HBM) for v in (weights, *features)]
    blocks = [pltpu.VMEM((4, ROWS, 512), BF16)] * 8
    key_value = call(
        key_value_kernel,
        shape((16, 4, 8, BLOCK), BF16),
        (where, *kept, taps),
        [pltpu.VMEM((4, 8, 2, 2, 64, 128), BF16)]
        + blocks
        + [pltpu.VMEM((4 * ROWS, 256), F32), pltpu.SemaphoreType.DMA((9,))],
        in_specs=[smem] + [anywhere] * 9 + [whole],
        flops=2 * 544 * 4096 * 256,
    )
    owned = exchanged(key_value, ("x", "yh"))
    key_value, taps = lax.optimization_barrier((key_value, taps))
    query = call(
        query_kernel,
        shape((2, 2, BLOCK, 128), BF16),
        (where, *kept, taps),
        [pltpu.VMEM((4, 8, 2, 64, 128), BF16)]
        + blocks
        + [pltpu.VMEM((4 * ROWS, 128), F32), pltpu.SemaphoreType.DMA((9,))],
        in_specs=[smem] + [anywhere] * 9 + [whole],
        flops=2 * 544 * 4096 * 128,
    )
    near = swapped(query[1], ("yl",), 1)
    tables, turns = dft_tables()
    filters, _ = lax.optimization_barrier((filters, key_value))
    spec, tables, turns = call(
        filter_kernel,
        (shape((8 * POINTS, 2 * POINTS), F32), shape(tables.shape, BF16), shape(turns.shape, F32)),
        (filters, tables, turns),
        (pltpu.VMEM((512, POINTS), F32),),
    )
    owned, near, spec = lax.optimization_barrier((owned, near, spec))
    far = swapped(jnp.stack([query[0, 1], near[1]]), ("z_hi",), 1)
    mixed = call(
        conv_kernel,
        shape((64, 8, BLOCK), BF16),
        (owned.reshape(16, 2, 2, 8, BLOCK), spec, skip_gain, tables, turns),
        (pltpu.VMEM((512, POINTS), F32), pltpu.VMEM((512, POINTS), F32)),
        in_specs=[whole, whole, smem, whole, whole],
        flops=2 * 168 * 10**6,
    )
    returned = exchanged(mixed, TOK)
    return call(
        gate_kernel,
        shape((BLOCK, 512), BF16),
        (where, query, near, far, returned),
        in_specs=[smem] + [whole] * 4,
    )


def solution(mesh):
    fine = Mesh(mesh.devices.reshape(SIZES), AXES)
    in_specs = (
        P(TOK, TP),
        P(TOK, TP),
        P(TOK, TP),
        P(TOK, TP),
        P(None, None, TP),
        P(TP + TOK, None),
        P(TP + TOK),
    )
    return jax.shard_map(mixer, mesh=fine, in_specs=in_specs, out_specs=P(TOK, TP), check_vma=False)
```

```python
import math

import jax
import jax.numpy as jnp
import numpy as np
from jax import lax
from jax.experimental import pallas as pl
from jax.experimental.pallas import tpu as pltpu
from jax.sharding import Mesh
from jax.sharding import PartitionSpec as P

AXES = ("z_hi", "x", "yh", "yl", "z_lo", "core")
SIZES = (2, 4, 4, 2, 4, 2)
TOK = AXES[:4]
TP = AXES[4:]
HALO = 8
BLOCK = 128
ROWS = HALO + BLOCK
POINTS = 128
F32 = jnp.float32
BF16 = jnp.bfloat16


def exchanged(value, axes):
    return lax.all_to_all(value, axes, split_axis=0, concat_axis=0, tiled=True)


def from_everyone(value, axes, apart=()):
    count = math.prod(SIZES[AXES.index(a)] for a in axes)
    copies = jnp.broadcast_to(value, (count, *value.shape))
    if apart:
        copies = copies.reshape(-1, *value.shape[1:])
    return exchanged(copies, axes + apart)


def dft_tables():
    n = np.arange(POINTS)
    full = 2.0 * np.pi * (np.outer(n, n) % POINTS) / POINTS
    cos, sin = np.cos(full), np.sin(full)
    half = POINTS // 2
    outer = np.concatenate([cos, -sin], axis=0)
    outer = np.concatenate([outer, outer], axis=1)
    inner = np.block([[cos, -sin], [sin, cos]])
    back_inner = np.block([[cos, sin], [-sin, cos]])
    back_outer = np.concatenate([cos[:half], -sin[:half]], axis=1) / POINTS**2
    twist = 2.0 * np.pi * np.outer(n, n) / POINTS**2
    tables = np.concatenate([inner, back_inner, outer, back_outer], axis=0)
    turns = np.concatenate([np.cos(twist), np.sin(twist)], axis=0)
    return jnp.asarray(tables, F32).astype(BF16), jnp.asarray(turns, F32)


def dot(a, b):
    return jnp.dot(a, b, preferred_element_type=F32)


def spectrum(rows, tables, turns):
    cos, sin = turns[0:POINTS], turns[POINTS:]
    blocks = jnp.concatenate(
        [rows[pl.ds(c, 64, stride=8), :].astype(BF16) for c in range(8)], axis=1
    )
    first = dot(tables[512:768, 0:64], blocks)
    turned = []
    for c in range(8):
        re = first[:POINTS, c * POINTS : (c + 1) * POINTS]
        im = first[POINTS:, c * POINTS : (c + 1) * POINTS]
        turned.append(
            jnp.concatenate([re * cos + im * sin, im * cos - re * sin], axis=1).astype(BF16)
        )
    return dot(jnp.concatenate(turned, axis=0), tables[0:256])


def filter_kernel(filters, tables, turns, spec, tables_out, turns_out, rows):
    tables_out[...] = tables[...]
    turns_out[...] = turns[...]
    taps = filters[...]
    unit = taps / jnp.sqrt(jnp.sum(taps * taps, axis=1, keepdims=True) + 1e-06)
    for b in range(64):
        rows[pl.ds(b * 8, 8), :] = unit[:, b * POINTS : (b + 1) * POINTS]
    spec[...] = spectrum(rows, tables, turns)


def conv_kernel(signal, spec, skip, tables, turns, mixed, rows, out):
    for z in range(2):
        rows[pl.ds(z * 256, 256), :] = signal[:, z].astype(F32).reshape(256, POINTS)
    cos, sin = turns[0:POINTS], turns[POINTS:]
    sig = spectrum(rows, tables, turns)
    re, im = sig[:, :POINTS], sig[:, POINTS:]
    f_re, f_im = spec[:, :POINTS], spec[:, POINTS:]
    prod = jnp.concatenate([re * f_re - im * f_im, re * f_im + im * f_re], axis=1)
    back = dot(prod.astype(BF16), tables[256:512])
    turned = []
    for c in range(8):
        b_re = back[c * POINTS : (c + 1) * POINTS, :POINTS]
        b_im = back[c * POINTS : (c + 1) * POINTS, POINTS:]
        turned.append(
            jnp.concatenate([b_re * cos - b_im * sin, b_re * sin + b_im * cos], axis=0).astype(BF16)
        )
    result = dot(tables[768:832], jnp.concatenate(turned, axis=1))
    for c in range(8):
        piece = result[:, c * POINTS : (c + 1) * POINTS]
        out[pl.ds(c, 64, stride=8), :] = piece + skip[c] * rows[pl.ds(c, 64, stride=8), :]
    mixed[...] = out[...].astype(BF16).reshape(64, 8, POINTS)


def order_table(rows_are_natural, mine=0):
    shape = (512, 512)
    row = lax.broadcasted_iota(jnp.int32, shape, 0)
    col = lax.broadcasted_iota(jnp.int32, shape, 1)
    grouped, natural = (col, row) if rows_are_natural else (row, col)
    quarter, xy, j = (grouped // 128) ^ mine, (grouped // 8) % 16, grouped % 8
    place = (quarter // 2) * 256 + xy * 16 + (quarter % 2) * 8 + j
    return (natural == place).astype(F32).astype(BF16)


def weights_kernel(where, w_key, w_value, w_query, mine, theirs, held, sems):
    copies = fetched((w_key, w_value, w_query), [held.at[p] for p in range(3)], sems)
    table = order_table(True)
    lower = where[2] < 2
    for p in range(3):
        copies[p].wait()
        cols = dot(held[p], table)
        ours = jnp.where(lower, cols[:, :256], cols[:, 256:]).astype(BF16)
        others = jnp.where(lower, cols[:, 256:], cols[:, :256]).astype(BF16)
        for yl in range(2):
            mine[yl, p] = ours[:, yl * 128 : (yl + 1) * 128]
            theirs[yl, p] = others[:, yl * 128 : (yl + 1) * 128]


def fetched(sources, held, sems):
    copies = [pltpu.make_async_copy(a, b, sems.at[i]) for i, (a, b) in enumerate(zip(sources, held))]
    for copy in copies:
        copy.start()
    return copies


def projected(where, features, w, acc, ready):
    for i, (half, low) in enumerate((h, l) for h in range(2) for l in (0, 2, 1, 3)):
        if i % 2 == 0:
            for copy in ready(i // 2):
                copy.wait()
        pieces = [
            features[half * 4 + parity * 2 + low % 2][(low // 2) * 2 : (low // 2) * 2 + 2]
            for parity in range(2)
        ]
        rows = jnp.concatenate([p.reshape(2 * ROWS, 512) for p in pieces], axis=0)
        term = dot(rows, w(i // 2, part_of(where, half, low)))
        if i == 0:
            acc[...] = term
        else:
            acc[...] += term


def part_of(where, half, low):
    return ((where[0] ^ low) & 3) * 2 + (where[1] ^ half)


def group_of(where, i):
    return ((i % 2) * 2 + i // 2) ^ where[2]


def short(acc, group, at, taps):
    top = group * ROWS + HALO
    cols = pl.ds(at, 128)
    return (
        taps[0:1] * acc[pl.ds(top, BLOCK), cols]
        + taps[1:2] * acc[pl.ds(top - 1, BLOCK), cols]
        + taps[2:3] * acc[pl.ds(top - 2, BLOCK), cols]
    )


def key_value_kernel(where, *refs):
    sources, (taps, out), (w, *held), (acc, sems) = refs[:9], refs[9:11], refs[11:20], refs[20:]
    pairs = [(half, low) for half in range(2) for low in range(2)]
    columns = [sources[0].at[part_of(where, half, low) & 3] for half, low in pairs]
    order = [half * 4 + parity * 2 + low for half, low in pairs for parity in range(2)]
    froms, targets = [], []
    for j in range(4):
        froms += [columns[j], sources[1 + order[2 * j]], sources[1 + order[2 * j + 1]]]
        targets += [w.at[j], held[order[2 * j]], held[order[2 * j + 1]]]
    copies = fetched(froms, targets, sems)

    def weights(j, part):
        z_hi = (part >> 2) ^ where[3]
        return jnp.concatenate([w[j, :, p, z_hi].reshape(512, 128) for p in range(2)], axis=1)

    projected(where, held, weights, acc, lambda j: copies[3 * j : 3 * j + 3])
    for i in range(4):
        keyed = short(acc, i, 0, taps[1])
        valued = short(acc, i, 128, taps[2])
        out[:, group_of(where, i)] = (keyed * valued).T.reshape(16, 8, BLOCK).astype(BF16)


def query_kernel(where, *refs):
    sources, (taps, out), (w, *held), (acc, sems) = refs[:12], refs[12:14], refs[14:23], refs[23:]
    copies = fetched(sources, [w.at[d] for d in range(4)] + held, sems)

    def weights(j, part):
        return w[(part & 3) ^ where[4], :, (part >> 2) ^ where[3]].reshape(512, 128)

    projected(where, held, weights, acc, lambda j: copies if j == 0 else [])
    for i in range(4):
        out[i // 2, i % 2] = short(acc, i, 0, taps[0]).astype(BF16)


def gate_kernel(where, query, near, far, returned, out):
    cols = jnp.concatenate([query[0, 0], near[0], far[0], far[1]], axis=1)
    natural = dot(cols, order_table(False, where[2]))
    mixed = returned[...].astype(F32).reshape(512, BLOCK).T
    out[...] = (natural * mixed).astype(BF16)


def call(kernel, out_shape, args, scratch=(), in_specs=None, flops=10**8):
    whole = pl.BlockSpec(memory_space=pltpu.VMEM)
    specs = in_specs or [whole] * len(args)
    moved = sum(math.prod(a.shape) * a.dtype.itemsize for a in args)
    return pl.pallas_call(
        kernel,
        out_shape=out_shape,
        in_specs=specs,
        out_specs=jax.tree.map(lambda _: whole, out_shape),
        scratch_shapes=list(scratch),
        compiler_params=pltpu.CompilerParams(vmem_limit_bytes=20 * 2**20),
        cost_estimate=pl.CostEstimate(flops=flops, bytes_accessed=moved, transcendentals=0),
    )(*args)


def of_previous(value, axes):
    count = math.prod(SIZES[AXES.index(a)] for a in axes)
    return lax.ppermute(value, axes, [(i, i + 1) for i in range(count - 1)])


def swapped(value, axes, bits):
    count = math.prod(SIZES[AXES.index(a)] for a in axes)
    return lax.ppermute(value, axes, [(i, i ^ bits) for i in range(count)])


def mixer(tokens, w_query, w_key, w_value, short_taps, filters, skip_gain):
    shape = jax.ShapeDtypeStruct
    whole = pl.BlockSpec(memory_space=pltpu.VMEM)
    smem = pl.BlockSpec(memory_space=pltpu.SMEM)
    place = lax.axis_index(AXES)
    core, z_lo, yl, x, z_hi = place % 2, place // 2 % 4, place // 8 % 2, place // 64 % 4, place // 256
    where = jnp.stack([z_hi * 4 + z_lo, core, z_hi * 2 + yl, z_hi, x])

    anywhere = pl.BlockSpec(memory_space=pl.ANY)
    halo = of_previous(tokens[-HALO:], TOK)
    part = shape((2, 3, 64, 128), BF16)
    own, others = call(
        weights_kernel,
        (part, part),
        (where, *(pltpu.with_memory_space_constraint(w, pltpu.HBM) for w in (w_key, w_value, w_query))),
        (pltpu.VMEM((3, 64, 512), BF16), pltpu.SemaphoreType.DMA((3,))),
        in_specs=[smem] + [anywhere] * 3,
    )
    others, halo = lax.optimization_barrier((others, halo))
    got = swapped(others, ("z_hi",), 1)
    first = from_everyone(jnp.stack([own, got], axis=2), ("yh",), ("yl",))

    ring = ("z_hi", "z_lo")
    mine = jnp.concatenate([halo, tokens], axis=0)[None]
    far_block = swapped(mine, ring, 4)
    two = jnp.concatenate([mine, far_block], axis=0)
    even = jnp.concatenate([two, swapped(two, ring, 2)], axis=0)
    taps = short_taps.reshape(3, 3, 2, 16, 2, 8)
    taps = lax.dynamic_index_in_dim(taps, z_hi, 2, keepdims=False)
    taps = lax.dynamic_index_in_dim(taps, yl, 3, keepdims=False).reshape(3, 3, 128)

    first, taps, where, _ = lax.optimization_barrier((first, taps, where, even))
    weights = from_everyone(first[:, :2], ("x",))
    odd = swapped(even, ring, 1)
    even_y = swapped(even, ("yl",), 1)
    odd_y = swapped(odd, ("yl",), 1)
    ours = (even, odd, even_y, odd_y)
    features = [swapped(v, ("core",), 1) for v in ours[:3]]
    features.append(swapped(odd_y, ("core",), 1))
    features = (*ours, *features)
    query_weights = [first[:, 2]]
    query_weights += [swapped(query_weights[0], ("x",), d) for d in (1, 2, 3)]

    kept = [pltpu.with_memory_space_constraint(v, pltpu.HBM) for v in features]
    blocks = [pltpu.VMEM((4, ROWS, 512), BF16)] * 8
    key_value = call(
        key_value_kernel,
        shape((16, 4, 8, BLOCK), BF16),
        (where, weights, *kept, taps),
        [pltpu.VMEM((4, 8, 2, 2, 64, 128), BF16)]
        + blocks
        + [pltpu.VMEM((4 * ROWS, 256), F32), pltpu.SemaphoreType.DMA((12,))],
        in_specs=[smem] + [anywhere] * 9 + [whole],
        flops=2 * 544 * 4096 * 256,
    )
    owned = exchanged(key_value, ("x", "yh"))
    key_value, taps = lax.optimization_barrier((key_value, taps))
    query = call(
        query_kernel,
        shape((2, 2, BLOCK, 128), BF16),
        (where, *query_weights, *kept, taps),
        [pltpu.VMEM((4, 8, 2, 64, 128), BF16)]
        + blocks
        + [pltpu.VMEM((4 * ROWS, 128), F32), pltpu.SemaphoreType.DMA((12,))],
        in_specs=[smem] + [anywhere] * 12 + [whole],
        flops=2 * 544 * 4096 * 128,
    )
    near = swapped(query[1], ("yl",), 1)
    tables, turns = dft_tables()
    filters, _ = lax.optimization_barrier((filters, key_value))
    spec, tables, turns = call(
        filter_kernel,
        (shape((8 * POINTS, 2 * POINTS), F32), shape(tables.shape, BF16), shape(turns.shape, F32)),
        (filters, tables, turns),
        (pltpu.VMEM((512, POINTS), F32),),
    )
    owned, near, spec = lax.optimization_barrier((owned, near, spec))
    far = swapped(jnp.stack([query[0, 1], near[1]]), ("z_hi",), 1)
    mixed = call(
        conv_kernel,
        shape((64, 8, BLOCK), BF16),
        (owned.reshape(16, 2, 2, 8, BLOCK), spec, skip_gain, tables, turns),
        (pltpu.VMEM((512, POINTS), F32), pltpu.VMEM((512, POINTS), F32)),
        in_specs=[whole, whole, smem, whole, whole],
        flops=2 * 168 * 10**6,
    )
    returned = exchanged(mixed, TOK)
    return call(
        gate_kernel, shape((BLOCK, 512), BF16), (where, query, near, far, returned), in_specs=[smem] + [whole] * 4
    )


def solution(mesh):
    fine = Mesh(mesh.devices.reshape(SIZES), AXES)
    in_specs = (
        P(TOK, TP),
        P(TOK, TP),
        P(TOK, TP),
        P(TOK, TP),
        P(None, None, TP),
        P(TP + TOK, None),
        P(TP + TOK),
    )
    return jax.shard_map(mixer, mesh=fine, in_specs=in_specs, out_specs=P(TOK, TP), check_vma=False)
```

```python
import math

import jax
import jax.numpy as jnp
import numpy as np
from jax import lax
from jax.experimental import pallas as pl
from jax.experimental.pallas import tpu as pltpu
from jax.sharding import Mesh
from jax.sharding import PartitionSpec as P

AXES = ("z_hi", "x", "yh", "yl", "z_lo", "core")
SIZES = (2, 4, 4, 2, 4, 2)
TOK = AXES[:4]
TP = AXES[4:]
HALO = 8
BLOCK = 128
ROWS = HALO + BLOCK
POINTS = 128
WEIGHT_TILES = 2 * 3 * 8
F32 = jnp.float32
BF16 = jnp.bfloat16


def exchanged(value, axes):
    return lax.all_to_all(value, axes, split_axis=0, concat_axis=0, tiled=True)


def from_everyone(value, axes, apart=()):
    count = math.prod(SIZES[AXES.index(a)] for a in axes)
    copies = jnp.broadcast_to(value, (count, *value.shape))
    if apart:
        copies = copies.reshape(-1, *value.shape[1:])
    return exchanged(copies, axes + apart)


def dft_tables():
    n = np.arange(POINTS)
    full = 2.0 * np.pi * (np.outer(n, n) % POINTS) / POINTS
    cos, sin = np.cos(full), np.sin(full)
    half = POINTS // 2
    outer = np.concatenate([cos, -sin], axis=0)
    outer = np.concatenate([outer, outer], axis=1)
    inner = np.block([[cos, -sin], [sin, cos]])
    back_inner = np.block([[cos, sin], [-sin, cos]])
    back_outer = np.concatenate([cos[:half], -sin[:half]], axis=1) / POINTS**2
    twist = 2.0 * np.pi * np.outer(n, n) / POINTS**2
    tables = np.concatenate([inner, back_inner, outer, back_outer], axis=0)
    turns = np.concatenate([np.cos(twist), np.sin(twist)], axis=0)
    return jnp.asarray(tables, F32).astype(BF16), jnp.asarray(turns, F32)


def dot(a, b):
    return jnp.dot(a, b, preferred_element_type=F32)


def spectrum(rows, tables, turns):
    cos, sin = turns[0:POINTS], turns[POINTS:]
    blocks = jnp.concatenate(
        [rows[pl.ds(c, 64, stride=8), :].astype(BF16) for c in range(8)], axis=1
    )
    first = dot(tables[512:768, 0:64], blocks)
    turned = []
    for c in range(8):
        re = first[:POINTS, c * POINTS : (c + 1) * POINTS]
        im = first[POINTS:, c * POINTS : (c + 1) * POINTS]
        turned.append(
            jnp.concatenate([re * cos + im * sin, im * cos - re * sin], axis=1).astype(BF16)
        )
    return dot(jnp.concatenate(turned, axis=0), tables[0:256])


def filter_kernel(filters, tables, turns, spec, tables_out, turns_out, rows):
    tables_out[...] = tables[...]
    turns_out[...] = turns[...]
    taps = filters[...]
    unit = taps / jnp.sqrt(jnp.sum(taps * taps, axis=1, keepdims=True) + 1e-06)
    for b in range(64):
        rows[pl.ds(b * 8, 8), :] = unit[:, b * POINTS : (b + 1) * POINTS]
    spec[...] = spectrum(rows, tables, turns)


def conv_kernel(signal, spec, skip, tables, turns, mixed, rows, out):
    for z in range(2):
        rows[pl.ds(z * 256, 256), :] = signal[:, z].astype(F32).reshape(256, POINTS)
    cos, sin = turns[0:POINTS], turns[POINTS:]
    sig = spectrum(rows, tables, turns)
    re, im = sig[:, :POINTS], sig[:, POINTS:]
    f_re, f_im = spec[:, :POINTS], spec[:, POINTS:]
    prod = jnp.concatenate([re * f_re - im * f_im, re * f_im + im * f_re], axis=1)
    back = dot(prod.astype(BF16), tables[256:512])
    turned = []
    for c in range(8):
        b_re = back[c * POINTS : (c + 1) * POINTS, :POINTS]
        b_im = back[c * POINTS : (c + 1) * POINTS, POINTS:]
        turned.append(
            jnp.concatenate([b_re * cos - b_im * sin, b_re * sin + b_im * cos], axis=0).astype(BF16)
        )
    result = dot(tables[768:832], jnp.concatenate(turned, axis=1))
    for c in range(8):
        piece = result[:, c * POINTS : (c + 1) * POINTS]
        out[pl.ds(c, 64, stride=8), :] = piece + skip[c] * rows[pl.ds(c, 64, stride=8), :]
    for z in range(2):
        mixed[:, z] = out[pl.ds(z * 256, 256), :].astype(BF16).reshape(16, 2, 8, POINTS)


def order_table(rows_are_natural):
    shape = (512, 512)
    row = lax.broadcasted_iota(jnp.int32, shape, 0)
    col = lax.broadcasted_iota(jnp.int32, shape, 1)
    grouped, natural = (col, row) if rows_are_natural else (row, col)
    quarter, xy, j = grouped // 128, (grouped // 8) % 16, grouped % 8
    place = (quarter // 2) * 256 + xy * 16 + (quarter % 2) * 8 + j
    return (natural == place).astype(F32).astype(BF16)


def first_kernel(where, w_key, w_value, w_query, tokens, halo, mine, sent, held, sems):
    copies = fetched((w_key, w_value, w_query), [held.at[p] for p in range(3)], sems)
    for k in range(4):
        cols = pl.ds(k * 128, 128)
        at = WEIGHT_TILES + k * ROWS // 8
        sent[at : at + 1] = halo[:, cols].astype(F32).reshape(1, 8, 128).astype(BF16)
        sent[at + 1 : at + 17] = tokens[:, cols].astype(F32).reshape(16, 8, 128).astype(BF16)
    table = order_table(True)
    lower = where[2] < 2
    for p in range(3):
        copies[p].wait()
        cols = dot(held[p], table)
        ours = jnp.where(lower, cols[:, :256], cols[:, 256:])
        others = jnp.where(lower, cols[:, 256:], cols[:, :256])
        for yl in range(2):
            mine[yl, p] = ours[:, yl * 128 : (yl + 1) * 128].astype(BF16)
            at = (yl * 3 + p) * 8
            sent[at : at + 8] = others[:, yl * 128 : (yl + 1) * 128].reshape(8, 8, 128).astype(BF16)


def fetched(sources, held, sems):
    copies = [pltpu.make_async_copy(a, b, sems.at[i]) for i, (a, b) in enumerate(zip(sources, held))]
    for copy in copies:
        copy.start()
    return copies


def projected(where, features, w, acc, ready):
    for i, (half, low) in enumerate((h, l) for h in range(2) for l in (0, 2, 1, 3)):
        if i % 2 == 0:
            for copy in ready(i // 2):
                copy.wait()
        pieces = [
            features[half * 4 + parity * 2 + low % 2][(low // 2) * 2 : (low // 2) * 2 + 2]
            for parity in range(2)
        ]
        pieces = [
            jnp.concatenate([p[:, k].reshape(2 * ROWS, 128) for k in range(4)], axis=1) for p in pieces
        ]
        rows = jnp.concatenate(pieces, axis=0)
        term = dot(rows, w(i // 2, part_of(where, half, low)))
        if i == 0:
            acc[...] = term
        else:
            acc[...] += term


def part_of(where, half, low):
    return ((where[0] ^ low) & 3) * 2 + (where[1] ^ half)


def group_of(where, i):
    return ((i % 2) * 2 + i // 2) ^ where[2]


def short(acc, group, at, taps):
    top = group * ROWS + HALO
    cols = pl.ds(at, 128)
    return (
        taps[0:1] * acc[pl.ds(top, BLOCK), cols]
        + taps[1:2] * acc[pl.ds(top - 1, BLOCK), cols]
        + taps[2:3] * acc[pl.ds(top - 2, BLOCK), cols]
    )


def key_value_kernel(where, *refs):
    sources, (taps, out), (w, *held), (acc, sems) = refs[:9], refs[9:11], refs[11:20], refs[20:]
    pairs = [(half, low) for half in range(2) for low in range(2)]
    columns = [sources[0].at[part_of(where, half, low) & 3] for half, low in pairs]
    order = [half * 4 + parity * 2 + low for half, low in pairs for parity in range(2)]
    froms, targets = [], []
    for j in range(4):
        froms += [columns[j], sources[1 + order[2 * j]], sources[1 + order[2 * j + 1]]]
        targets += [w.at[j], held[order[2 * j]], held[order[2 * j + 1]]]
    copies = fetched(froms, targets, sems)

    def weights(j, part):
        z_hi = (part >> 2) ^ where[3]
        return jnp.concatenate([w[j, :, p, z_hi].reshape(512, 128) for p in range(2)], axis=1)

    projected(where, held, weights, acc, lambda j: copies[3 * j : 3 * j + 3])
    for i in range(4):
        keyed = short(acc, i, 0, taps[1])
        valued = short(acc, i, 128, taps[2])
        out[:, group_of(where, i)] = (keyed * valued).T.reshape(16, 8, BLOCK).astype(BF16)


def query_kernel(where, *refs):
    sources, (taps, out), (w, *held), (acc, sems) = refs[:10], refs[10:12], refs[12:21], refs[21:]
    copies = fetched(sources, [w.at[0:2], w.at[2:4]] + held, sems)

    def weights(j, part):
        return w[(part & 3) ^ where[4], :, (part >> 2) ^ where[3]].reshape(512, 128)

    projected(where, held, weights, acc, lambda j: copies if j == 0 else [])
    for i in range(4):
        out[group_of(where, i)] = short(acc, i, 0, taps[0]).astype(BF16)


def gate_kernel(query, returned, out):
    for group in range(4):
        mixed = returned[:, group].astype(F32).reshape(128, BLOCK).T
        out[group] = (query[group].astype(F32) * mixed).astype(BF16)


def order_kernel(gated, out):
    cols = jnp.concatenate([gated[g] for g in range(4)], axis=1)
    out[...] = dot(cols, order_table(False)).astype(BF16)


def call(kernel, out_shape, args, scratch=(), in_specs=None, flops=10**8):
    whole = pl.BlockSpec(memory_space=pltpu.VMEM)
    specs = in_specs or [whole] * len(args)
    moved = sum(math.prod(a.shape) * a.dtype.itemsize for a in args)
    return pl.pallas_call(
        kernel,
        out_shape=out_shape,
        in_specs=specs,
        out_specs=jax.tree.map(lambda _: whole, out_shape),
        scratch_shapes=list(scratch),
        compiler_params=pltpu.CompilerParams(vmem_limit_bytes=20 * 2**20),
        cost_estimate=pl.CostEstimate(flops=flops, bytes_accessed=moved, transcendentals=0),
    )(*args)


def of_previous(value, axes):
    count = math.prod(SIZES[AXES.index(a)] for a in axes)
    return lax.ppermute(value, axes, [(i, i + 1) for i in range(count - 1)])


def swapped(value, axes, bits):
    count = math.prod(SIZES[AXES.index(a)] for a in axes)
    return lax.ppermute(value, axes, [(i, i ^ bits) for i in range(count)])


def mixer(tokens, w_query, w_key, w_value, short_taps, filters, skip_gain):
    shape = jax.ShapeDtypeStruct
    whole = pl.BlockSpec(memory_space=pltpu.VMEM)
    smem = pl.BlockSpec(memory_space=pltpu.SMEM)
    place = lax.axis_index(AXES)
    core, z_lo, yl, x, z_hi = place % 2, place // 2 % 4, place // 8 % 2, place // 64 % 4, place // 256
    where = jnp.stack([z_hi * 4 + z_lo, core, z_hi * 2 + yl, z_hi, x])

    anywhere = pl.BlockSpec(memory_space=pl.ANY)
    halo = of_previous(tokens[-HALO:], TOK)
    own, sent = call(
        first_kernel,
        (shape((2, 3, 64, 128), BF16), shape((WEIGHT_TILES + 4 * ROWS // 8, 8, 128), BF16)),
        (
            where,
            *(pltpu.with_memory_space_constraint(w, pltpu.HBM) for w in (w_key, w_value, w_query)),
            tokens,
            halo,
        ),
        (pltpu.VMEM((3, 64, 512), BF16), pltpu.SemaphoreType.DMA((3,))),
        in_specs=[smem] + [anywhere] * 3 + [whole] * 2,
    )
    ring = ("z_hi", "z_lo")
    got = swapped(sent, ring, 4)
    got_weights = got[:WEIGHT_TILES].reshape(2, 3, 64, 128)
    first = from_everyone(jnp.stack([own, got_weights], axis=2), ("yh",), ("yl",))

    two = jnp.stack([v[WEIGHT_TILES:].reshape(4, ROWS, 128) for v in (sent, got)])
    even = jnp.concatenate([two, swapped(two, ring, 2)], axis=0)

    taps = short_taps.reshape(3, 3, 2, 16, 2, 8)
    taps = lax.dynamic_index_in_dim(taps, z_hi, 2, keepdims=False)
    taps = lax.dynamic_index_in_dim(taps, yl, 3, keepdims=False).reshape(3, 3, 128)

    first, taps, where, _ = lax.optimization_barrier((first, taps, where, even))
    weights = from_everyone(first[:, :2], ("x",))
    odd = swapped(even, ring, 1)
    even_y = swapped(even, ("yl",), 1)
    odd_y = swapped(odd, ("yl",), 1)
    ours = (even, odd, even_y, odd_y)
    features = [swapped(v, ("core",), 1) for v in ours]
    features = (*ours, *features)
    half_weights, last = lax.optimization_barrier((first[:, 2], features[-1]))
    features = (*features[:-1], last)
    half_weights = jnp.stack([half_weights, swapped(half_weights, ("x",), 1)])
    query_weights = [half_weights, swapped(half_weights, ("x",), 2)]

    kept = [pltpu.with_memory_space_constraint(v, pltpu.HBM) for v in features]
    blocks = [pltpu.VMEM((4, 4, ROWS, 128), BF16)] * 8
    key_value = call(
        key_value_kernel,
        shape((16, 4, 8, BLOCK), BF16),
        (where, weights, *kept, taps),
        [pltpu.VMEM((4, 8, 2, 2, 64, 128), BF16)]
        + blocks
        + [pltpu.VMEM((4 * ROWS, 256), F32), pltpu.SemaphoreType.DMA((12,))],
        in_specs=[smem] + [anywhere] * 9 + [whole],
        flops=2 * 544 * 4096 * 256,
    )
    owned = exchanged(key_value, ("x", "yh"))
    tables, turns = dft_tables()
    filters, _ = lax.optimization_barrier((filters, key_value))
    spec, tables, turns = call(
        filter_kernel,
        (shape((8 * POINTS, 2 * POINTS), F32), shape(tables.shape, BF16), shape(turns.shape, F32)),
        (filters, tables, turns),
        (pltpu.VMEM((512, POINTS), F32),),
    )
    owned, spec = lax.optimization_barrier((owned, spec))
    mixed = call(
        conv_kernel,
        shape((16, 2, 2, 8, BLOCK), BF16),
        (owned.reshape(16, 2, 2, 8, BLOCK), spec, skip_gain, tables, turns),
        (pltpu.VMEM((512, POINTS), F32), pltpu.VMEM((512, POINTS), F32)),
        in_specs=[whole, whole, smem, whole, whole],
        flops=2 * 168 * 10**6,
    )
    returned = exchanged(mixed.reshape(16, 4, 8, BLOCK), ("x", "yh"))
    taps, _ = lax.optimization_barrier((taps, mixed))
    query = call(
        query_kernel,
        shape((4, BLOCK, 128), BF16),
        (where, *(pltpu.with_memory_space_constraint(v, pltpu.HBM) for v in query_weights), *kept, taps),
        [pltpu.VMEM((4, 8, 2, 64, 128), BF16)]
        + blocks
        + [pltpu.VMEM((4 * ROWS, 128), F32), pltpu.SemaphoreType.DMA((10,))],
        in_specs=[smem] + [anywhere] * 10 + [whole],
        flops=2 * 544 * 4096 * 128,
    )
    gated = call(gate_kernel, shape((4, BLOCK, 128), BF16), (query, returned))
    gated = exchanged(gated, ("z_hi", "yl"))
    return call(order_kernel, shape((BLOCK, 512), BF16), (gated,))


def solution(mesh):
    fine = Mesh(mesh.devices.reshape(SIZES), AXES)
    in_specs = (
        P(TOK, TP),
        P(TOK, TP),
        P(TOK, TP),
        P(TOK, TP),
        P(None, None, TP),
        P(TP + TOK, None),
        P(TP + TOK),
    )
    return jax.shard_map(mixer, mesh=fine, in_specs=in_specs, out_specs=P(TOK, TP), check_vma=False)
```

```python
import math

import jax
import jax.numpy as jnp
import numpy as np
from jax import lax
from jax.experimental import pallas as pl
from jax.experimental.pallas import tpu as pltpu
from jax.sharding import Mesh
from jax.sharding import PartitionSpec as P

AXES = ("z_hi", "x", "yh", "yl", "z_lo", "core")
SIZES = (2, 4, 4, 2, 4, 2)
TOK = AXES[:4]
TP = AXES[4:]
HALO = 8
BLOCK = 128
ROWS = HALO + BLOCK
POINTS = 128
F32 = jnp.float32
BF16 = jnp.bfloat16


def exchanged(value, axes):
    return lax.all_to_all(value, axes, split_axis=0, concat_axis=0, tiled=True)


def from_everyone(value, axes, apart=()):
    count = math.prod(SIZES[AXES.index(a)] for a in axes)
    copies = jnp.broadcast_to(value, (count, *value.shape))
    if apart:
        copies = copies.reshape(-1, *value.shape[1:])
    return exchanged(copies, axes + apart)


def dft_tables():
    n = np.arange(POINTS)
    full = 2.0 * np.pi * (np.outer(n, n) % POINTS) / POINTS
    cos, sin = np.cos(full), np.sin(full)
    half = POINTS // 2
    outer = np.concatenate([cos, -sin], axis=0)
    outer = np.concatenate([outer, outer], axis=1)
    inner = np.block([[cos, -sin], [sin, cos]])
    back_inner = np.block([[cos, sin], [-sin, cos]])
    back_outer = np.concatenate([cos[:half], -sin[:half]], axis=1) / POINTS**2
    twist = 2.0 * np.pi * np.outer(n, n) / POINTS**2
    tables = np.concatenate([inner, back_inner, outer, back_outer], axis=0)
    turns = np.concatenate([np.cos(twist), np.sin(twist)], axis=0)
    return jnp.asarray(tables, F32).astype(BF16), jnp.asarray(turns, F32)


def dot(a, b):
    return jnp.dot(a, b, preferred_element_type=F32)


def spectrum(rows, tables, turns):
    cos, sin = turns[0:POINTS], turns[POINTS:]
    blocks = jnp.concatenate(
        [rows[pl.ds(c, 64, stride=8), :].astype(BF16) for c in range(8)], axis=1
    )
    first = dot(tables[512:768, 0:64], blocks)
    turned = []
    for c in range(8):
        re = first[:POINTS, c * POINTS : (c + 1) * POINTS]
        im = first[POINTS:, c * POINTS : (c + 1) * POINTS]
        turned.append(
            jnp.concatenate([re * cos + im * sin, im * cos - re * sin], axis=1).astype(BF16)
        )
    return dot(jnp.concatenate(turned, axis=0), tables[0:256])


def filter_kernel(filters, tables, turns, spec, tables_out, turns_out, rows):
    tables_out[...] = tables[...]
    turns_out[...] = turns[...]
    taps = filters[...]
    unit = taps / jnp.sqrt(jnp.sum(taps * taps, axis=1, keepdims=True) + 1e-06)
    for b in range(64):
        rows[pl.ds(b * 8, 8), :] = unit[:, b * POINTS : (b + 1) * POINTS]
    spec[...] = spectrum(rows, tables, turns)


def conv_kernel(signal, spec, skip, tables, turns, mixed, rows, out):
    for z in range(2):
        rows[pl.ds(z * 256, 256), :] = signal[:, z].astype(F32).reshape(256, POINTS)
    cos, sin = turns[0:POINTS], turns[POINTS:]
    sig = spectrum(rows, tables, turns)
    re, im = sig[:, :POINTS], sig[:, POINTS:]
    f_re, f_im = spec[:, :POINTS], spec[:, POINTS:]
    prod = jnp.concatenate([re * f_re - im * f_im, re * f_im + im * f_re], axis=1)
    back = dot(prod.astype(BF16), tables[256:512])
    turned = []
    for c in range(8):
        b_re = back[c * POINTS : (c + 1) * POINTS, :POINTS]
        b_im = back[c * POINTS : (c + 1) * POINTS, POINTS:]
        turned.append(
            jnp.concatenate([b_re * cos - b_im * sin, b_re * sin + b_im * cos], axis=0).astype(BF16)
        )
    result = dot(tables[768:832], jnp.concatenate(turned, axis=1))
    for c in range(8):
        piece = result[:, c * POINTS : (c + 1) * POINTS]
        out[pl.ds(c, 64, stride=8), :] = piece + skip[c] * rows[pl.ds(c, 64, stride=8), :]
    for z in range(2):
        mixed[:, z] = out[pl.ds(z * 256, 256), :].astype(BF16).reshape(16, 2, 8, POINTS)


def order_table(rows_are_natural):
    shape = (512, 512)
    row = lax.broadcasted_iota(jnp.int32, shape, 0)
    col = lax.broadcasted_iota(jnp.int32, shape, 1)
    grouped, natural = (col, row) if rows_are_natural else (row, col)
    quarter, xy, j = grouped // 128, (grouped // 8) % 16, grouped % 8
    place = (quarter // 2) * 256 + xy * 16 + (quarter % 2) * 8 + j
    return (natural == place).astype(F32).astype(BF16)


def weights_kernel(where, w_key, w_value, w_query, mine, theirs, held, sems):
    copies = fetched((w_key, w_value, w_query), [held.at[p] for p in range(3)], sems)
    table = order_table(True)
    lower = where[2] < 2
    for p in range(3):
        copies[p].wait()
        cols = dot(held[p], table)
        ours = jnp.where(lower, cols[:, :256], cols[:, 256:]).astype(BF16)
        others = jnp.where(lower, cols[:, 256:], cols[:, :256]).astype(BF16)
        for yl in range(2):
            mine[yl, p] = ours[:, yl * 128 : (yl + 1) * 128]
            theirs[yl, p] = others[:, yl * 128 : (yl + 1) * 128]


def fetched(sources, held, sems):
    copies = [pltpu.make_async_copy(a, b, sems.at[i]) for i, (a, b) in enumerate(zip(sources, held))]
    for copy in copies:
        copy.start()
    return copies


def projected(where, features, w, acc, ready):
    for i, (half, low) in enumerate((h, l) for h in range(2) for l in (0, 2, 1, 3)):
        if i % 2 == 0:
            for copy in ready(i // 2):
                copy.wait()
        pieces = [
            features[half * 4 + parity * 2 + low % 2][(low // 2) * 2 : (low // 2) * 2 + 2]
            for parity in range(2)
        ]
        rows = jnp.concatenate([p.reshape(2 * ROWS, 512) for p in pieces], axis=0)
        term = dot(rows, w(i // 2, part_of(where, half, low)))
        if i == 0:
            acc[...] = term
        else:
            acc[...] += term


def part_of(where, half, low):
    return ((where[0] ^ low) & 3) * 2 + (where[1] ^ half)


def group_of(where, i):
    return ((i % 2) * 2 + i // 2) ^ where[2]


def short(acc, group, at, taps):
    top = group * ROWS + HALO
    cols = pl.ds(at, 128)
    return (
        taps[0:1] * acc[pl.ds(top, BLOCK), cols]
        + taps[1:2] * acc[pl.ds(top - 1, BLOCK), cols]
        + taps[2:3] * acc[pl.ds(top - 2, BLOCK), cols]
    )


def key_value_kernel(where, *refs):
    sources, (taps, out), (w, *held), (acc, sems) = refs[:9], refs[9:11], refs[11:20], refs[20:]
    pairs = [(half, low) for half in range(2) for low in range(2)]
    columns = [sources[0].at[part_of(where, half, low) & 3] for half, low in pairs]
    order = [half * 4 + parity * 2 + low for half, low in pairs for parity in range(2)]
    froms, targets = [], []
    for j in range(4):
        froms += [columns[j], sources[1 + order[2 * j]], sources[1 + order[2 * j + 1]]]
        targets += [w.at[j], held[order[2 * j]], held[order[2 * j + 1]]]
    copies = fetched(froms, targets, sems)

    def weights(j, part):
        z_hi = (part >> 2) ^ where[3]
        return jnp.concatenate([w[j, :, p, z_hi].reshape(512, 128) for p in range(2)], axis=1)

    projected(where, held, weights, acc, lambda j: copies[3 * j : 3 * j + 3])
    for i in range(4):
        keyed = short(acc, i, 0, taps[1])
        valued = short(acc, i, 128, taps[2])
        out[:, group_of(where, i)] = (keyed * valued).T.reshape(16, 8, BLOCK).astype(BF16)


def query_kernel(where, *refs):
    sources, (taps, out), (w, *held), (acc, sems) = refs[:12], refs[12:14], refs[14:23], refs[23:]
    copies = fetched(sources, [w.at[d] for d in range(4)] + held, sems)

    def weights(j, part):
        return w[(part & 3) ^ where[4], :, (part >> 2) ^ where[3]].reshape(512, 128)

    projected(where, held, weights, acc, lambda j: copies if j == 0 else [])
    for i in range(4):
        out[group_of(where, i)] = short(acc, i, 0, taps[0]).astype(BF16)


def gate_kernel(query, returned, out):
    for group in range(4):
        mixed = returned[:, group].astype(F32).reshape(128, BLOCK).T
        out[group] = (query[group].astype(F32) * mixed).astype(BF16)


def order_kernel(gated, out):
    cols = jnp.concatenate([gated[g] for g in range(4)], axis=1)
    out[...] = dot(cols, order_table(False)).astype(BF16)


def call(kernel, out_shape, args, scratch=(), in_specs=None, flops=10**8):
    whole = pl.BlockSpec(memory_space=pltpu.VMEM)
    specs = in_specs or [whole] * len(args)
    moved = sum(math.prod(a.shape) * a.dtype.itemsize for a in args)
    return pl.pallas_call(
        kernel,
        out_shape=out_shape,
        in_specs=specs,
        out_specs=jax.tree.map(lambda _: whole, out_shape),
        scratch_shapes=list(scratch),
        compiler_params=pltpu.CompilerParams(vmem_limit_bytes=20 * 2**20),
        cost_estimate=pl.CostEstimate(flops=flops, bytes_accessed=moved, transcendentals=0),
    )(*args)


def of_previous(value, axes):
    count = math.prod(SIZES[AXES.index(a)] for a in axes)
    return lax.ppermute(value, axes, [(i, i + 1) for i in range(count - 1)])


def swapped(value, axes, bits):
    count = math.prod(SIZES[AXES.index(a)] for a in axes)
    return lax.ppermute(value, axes, [(i, i ^ bits) for i in range(count)])


def mixer(tokens, w_query, w_key, w_value, short_taps, filters, skip_gain):
    shape = jax.ShapeDtypeStruct
    whole = pl.BlockSpec(memory_space=pltpu.VMEM)
    smem = pl.BlockSpec(memory_space=pltpu.SMEM)
    place = lax.axis_index(AXES)
    core, z_lo, yl, x, z_hi = place % 2, place // 2 % 4, place // 8 % 2, place // 64 % 4, place // 256
    where = jnp.stack([z_hi * 4 + z_lo, core, z_hi * 2 + yl, z_hi, x])

    anywhere = pl.BlockSpec(memory_space=pl.ANY)
    halo = of_previous(tokens[-HALO:], TOK)
    part = shape((2, 3, 64, 128), BF16)
    own, others = call(
        weights_kernel,
        (part, part),
        (where, *(pltpu.with_memory_space_constraint(w, pltpu.HBM) for w in (w_key, w_value, w_query))),
        (pltpu.VMEM((3, 64, 512), BF16), pltpu.SemaphoreType.DMA((3,))),
        in_specs=[smem] + [anywhere] * 3,
    )
    got = swapped(others, ("z_hi",), 1)
    first = from_everyone(jnp.stack([own, got], axis=2), ("yh",), ("yl",))

    ring = ("z_hi", "z_lo")
    mine = jnp.concatenate([halo, tokens], axis=0)[None]
    far_block = swapped(mine, ring, 4)
    two = jnp.concatenate([mine, far_block], axis=0)
    even = jnp.concatenate([two, swapped(two, ring, 2)], axis=0)
    taps = short_taps.reshape(3, 3, 2, 16, 2, 8)
    taps = lax.dynamic_index_in_dim(taps, z_hi, 2, keepdims=False)
    taps = lax.dynamic_index_in_dim(taps, yl, 3, keepdims=False).reshape(3, 3, 128)

    first, taps, where, _ = lax.optimization_barrier((first, taps, where, even))
    weights = from_everyone(first[:, :2], ("x",))
    odd = swapped(even, ring, 1)
    even_y = swapped(even, ("yl",), 1)
    odd_y = swapped(odd, ("yl",), 1)
    ours = (even, odd, even_y, odd_y)
    features = list(ours)
    for blocks in ours:
        features.append(swapped(blocks, ("core",), 1))
    slice_of_first, last = lax.optimization_barrier((first[:, 2], features[-1]))
    features = (*features[:-1], last)
    query_weights = [slice_of_first]
    query_weights += [swapped(query_weights[0], ("x",), d) for d in (1, 2, 3)]

    kept = [pltpu.with_memory_space_constraint(v, pltpu.HBM) for v in features]
    blocks = [pltpu.VMEM((4, ROWS, 512), BF16)] * 8
    key_value = call(
        key_value_kernel,
        shape((16, 4, 8, BLOCK), BF16),
        (where, weights, *kept, taps),
        [pltpu.VMEM((4, 8, 2, 2, 64, 128), BF16)]
        + blocks
        + [pltpu.VMEM((4 * ROWS, 256), F32), pltpu.SemaphoreType.DMA((12,))],
        in_specs=[smem] + [anywhere] * 9 + [whole],
        flops=2 * 544 * 4096 * 256,
    )
    owned = exchanged(key_value, ("x", "yh"))
    tables, turns = dft_tables()
    filters, _ = lax.optimization_barrier((filters, key_value))
    spec, tables, turns = call(
        filter_kernel,
        (shape((8 * POINTS, 2 * POINTS), F32), shape(tables.shape, BF16), shape(turns.shape, F32)),
        (filters, tables, turns),
        (pltpu.VMEM((512, POINTS), F32),),
    )
    owned, spec = lax.optimization_barrier((owned, spec))
    mixed = call(
        conv_kernel,
        shape((16, 2, 2, 8, BLOCK), BF16),
        (owned.reshape(16, 2, 2, 8, BLOCK), spec, skip_gain, tables, turns),
        (pltpu.VMEM((512, POINTS), F32), pltpu.VMEM((512, POINTS), F32)),
        in_specs=[whole, whole, smem, whole, whole],
        flops=2 * 168 * 10**6,
    )
    returned = exchanged(mixed.reshape(16, 4, 8, BLOCK), ("x", "yh"))
    taps, _ = lax.optimization_barrier((taps, mixed))
    query = call(
        query_kernel,
        shape((4, BLOCK, 128), BF16),
        (where, *query_weights, *kept, taps),
        [pltpu.VMEM((4, 8, 2, 64, 128), BF16)]
        + blocks
        + [pltpu.VMEM((4 * ROWS, 128), F32), pltpu.SemaphoreType.DMA((12,))],
        in_specs=[smem] + [anywhere] * 12 + [whole],
        flops=2 * 544 * 4096 * 128,
    )
    gated = call(gate_kernel, shape((4, BLOCK, 128), BF16), (query, returned))
    gated = exchanged(gated, ("z_hi", "yl"))
    return call(order_kernel, shape((BLOCK, 512), BF16), (gated,))


def solution(mesh):
    fine = Mesh(mesh.devices.reshape(SIZES), AXES)
    in_specs = (
        P(TOK, TP),
        P(TOK, TP),
        P(TOK, TP),
        P(TOK, TP),
        P(None, None, TP),
        P(TP + TOK, None),
        P(TP + TOK),
    )
    return jax.shard_map(mixer, mesh=fine, in_specs=in_specs, out_specs=P(TOK, TP), check_vma=False)
```

```python
import math

import jax
import jax.numpy as jnp
import numpy as np
from jax import lax
from jax.experimental import pallas as pl
from jax.experimental.pallas import tpu as pltpu
from jax.sharding import Mesh
from jax.sharding import PartitionSpec as P

AXES = ("z_hi", "x", "yh", "yl", "z_lo", "core")
SIZES = (2, 4, 4, 2, 4, 2)
TOK = AXES[:4]
TP = AXES[4:]
HALO = 8
BLOCK = 128
ROWS = HALO + BLOCK
POINTS = 128
F32 = jnp.float32
BF16 = jnp.bfloat16


def exchanged(value, axes):
    return lax.all_to_all(value, axes, split_axis=0, concat_axis=0, tiled=True)


def from_everyone(value, axes, apart=()):
    count = math.prod(SIZES[AXES.index(a)] for a in axes)
    copies = jnp.broadcast_to(value, (count, *value.shape))
    if apart:
        copies = copies.reshape(-1, *value.shape[1:])
    return exchanged(copies, axes + apart)


def dft_tables():
    n = np.arange(POINTS)
    full = 2.0 * np.pi * (np.outer(n, n) % POINTS) / POINTS
    cos, sin = np.cos(full), np.sin(full)
    half = POINTS // 2
    outer = np.concatenate([cos, -sin], axis=0)
    outer = np.concatenate([outer, outer], axis=1)
    inner = np.block([[cos, -sin], [sin, cos]])
    back_inner = np.block([[cos, sin], [-sin, cos]])
    back_outer = np.concatenate([cos[:half], -sin[:half]], axis=1) / POINTS**2
    twist = 2.0 * np.pi * np.outer(n, n) / POINTS**2
    tables = np.concatenate([inner, back_inner, outer, back_outer], axis=0)
    turns = np.concatenate([np.cos(twist), np.sin(twist)], axis=0)
    return jnp.asarray(tables, F32).astype(BF16), jnp.asarray(turns, F32)


def dot(a, b):
    return jnp.dot(a, b, preferred_element_type=F32)


def spectrum(rows, tables, turns):
    cos, sin = turns[0:POINTS], turns[POINTS:]
    blocks = jnp.concatenate(
        [rows[pl.ds(c, 64, stride=8), :].astype(BF16) for c in range(8)], axis=1
    )
    first = dot(tables[512:768, 0:64], blocks)
    turned = []
    for c in range(8):
        re = first[:POINTS, c * POINTS : (c + 1) * POINTS]
        im = first[POINTS:, c * POINTS : (c + 1) * POINTS]
        turned.append(
            jnp.concatenate([re * cos + im * sin, im * cos - re * sin], axis=1).astype(BF16)
        )
    return dot(jnp.concatenate(turned, axis=0), tables[0:256])


def filter_kernel(filters, tables, turns, spec, tables_out, turns_out, rows):
    tables_out[...] = tables[...]
    turns_out[...] = turns[...]
    taps = filters[...]
    unit = taps / jnp.sqrt(jnp.sum(taps * taps, axis=1, keepdims=True) + 1e-06)
    for b in range(64):
        rows[pl.ds(b * 8, 8), :] = unit[:, b * POINTS : (b + 1) * POINTS]
    spec[...] = spectrum(rows, tables, turns)


def conv_kernel(signal, spec, skip, tables, turns, mixed, rows, out):
    for z in range(2):
        rows[pl.ds(z * 256, 256), :] = signal[:, z].astype(F32).reshape(256, POINTS)
    cos, sin = turns[0:POINTS], turns[POINTS:]
    sig = spectrum(rows, tables, turns)
    re, im = sig[:, :POINTS], sig[:, POINTS:]
    f_re, f_im = spec[:, :POINTS], spec[:, POINTS:]
    prod = jnp.concatenate([re * f_re - im * f_im, re * f_im + im * f_re], axis=1)
    back = dot(prod.astype(BF16), tables[256:512])
    turned = []
    for c in range(8):
        b_re = back[c * POINTS : (c + 1) * POINTS, :POINTS]
        b_im = back[c * POINTS : (c + 1) * POINTS, POINTS:]
        turned.append(
            jnp.concatenate([b_re * cos - b_im * sin, b_re * sin + b_im * cos], axis=0).astype(BF16)
        )
    result = dot(tables[768:832], jnp.concatenate(turned, axis=1))
    for c in range(8):
        piece = result[:, c * POINTS : (c + 1) * POINTS]
        out[pl.ds(c, 64, stride=8), :] = piece + skip[c] * rows[pl.ds(c, 64, stride=8), :]
    for z in range(2):
        mixed[:, z] = out[pl.ds(z * 256, 256), :].astype(BF16).reshape(16, 2, 8, POINTS)


def order_table(rows_are_natural):
    shape = (512, 512)
    row = lax.broadcasted_iota(jnp.int32, shape, 0)
    col = lax.broadcasted_iota(jnp.int32, shape, 1)
    grouped, natural = (col, row) if rows_are_natural else (row, col)
    quarter, xy, j = grouped // 128, (grouped // 8) % 16, grouped % 8
    place = (quarter // 2) * 256 + xy * 16 + (quarter % 2) * 8 + j
    return (natural == place).astype(F32).astype(BF16)


def weights_kernel(where, w_key, w_value, w_query, mine, theirs, held, sems):
    copies = fetched((w_key, w_value, w_query), [held.at[p] for p in range(3)], sems)
    table = order_table(True)
    lower = where[2] < 2
    for p in range(3):
        copies[p].wait()
        cols = dot(held[p], table)
        ours = jnp.where(lower, cols[:, :256], cols[:, 256:]).astype(BF16)
        others = jnp.where(lower, cols[:, 256:], cols[:, :256]).astype(BF16)
        for yl in range(2):
            mine[yl, p] = ours[:, yl * 128 : (yl + 1) * 128]
            theirs[yl, p] = others[:, yl * 128 : (yl + 1) * 128]


def fetched(sources, held, sems):
    copies = [pltpu.make_async_copy(a, b, sems.at[i]) for i, (a, b) in enumerate(zip(sources, held))]
    for copy in copies:
        copy.start()
    return copies


def projected(where, features, w, acc, ready):
    for i, (half, low) in enumerate((h, l) for h in range(2) for l in (0, 2, 1, 3)):
        for copy in ready(i):
            copy.wait()
        kind = (low % 2) * 2 + low // 2
        pieces = [features[half * 8 + parity * 4 + kind][...] for parity in range(2)]
        rows = jnp.concatenate([p.reshape(2 * ROWS, 512) for p in pieces], axis=0)
        term = dot(rows, w(i // 2, part_of(where, half, low)))
        if i == 0:
            acc[...] = term
        else:
            acc[...] += term


def part_of(where, half, low):
    return ((where[0] ^ low) & 3) * 2 + (where[1] ^ half)


def group_of(where, i):
    return ((i % 2) * 2 + i // 2) ^ where[2]


def short(acc, group, at, taps):
    top = group * ROWS + HALO
    cols = pl.ds(at, 128)
    return (
        taps[0:1] * acc[pl.ds(top, BLOCK), cols]
        + taps[1:2] * acc[pl.ds(top - 1, BLOCK), cols]
        + taps[2:3] * acc[pl.ds(top - 2, BLOCK), cols]
    )


def key_value_kernel(where, *refs):
    sources, (taps, out), (w, *held), (acc, sems) = refs[:17], refs[17:19], refs[19:36], refs[36:]
    pairs = [(half, low) for half in range(2) for low in range(2)]
    columns = [sources[0].at[part_of(where, half, low) & 3] for half, low in pairs]
    froms, targets, needs = [], [], []
    for j, (half, low) in enumerate(pairs):
        for kind in (2 * low, 2 * low + 1):
            begin = len(froms)
            if kind % 2 == 0:
                froms.append(columns[j])
                targets.append(w.at[j])
            wanted = [half * 8 + parity * 4 + kind for parity in range(2)]
            froms += [sources[1 + k] for k in wanted]
            targets += [held[k] for k in wanted]
            needs.append(slice(begin, len(froms)))
    copies = fetched(froms, targets, sems)

    def weights(j, part):
        z_hi = (part >> 2) ^ where[3]
        return jnp.concatenate([w[j, :, p, z_hi].reshape(512, 128) for p in range(2)], axis=1)

    projected(where, held, weights, acc, lambda i: copies[needs[i]])
    for i in range(4):
        keyed = short(acc, i, 0, taps[1])
        valued = short(acc, i, 128, taps[2])
        out[:, group_of(where, i)] = (keyed * valued).T.reshape(16, 8, BLOCK).astype(BF16)


def query_kernel(where, *refs):
    sources, (taps, out), (w, *held), (acc, sems) = refs[:20], refs[20:22], refs[22:39], refs[39:]
    copies = fetched(sources, [w.at[d] for d in range(4)] + held, sems)

    def weights(j, part):
        return w[(part & 3) ^ where[4], :, (part >> 2) ^ where[3]].reshape(512, 128)

    projected(where, held, weights, acc, lambda i: copies if i == 0 else [])
    for i in range(4):
        out[group_of(where, i)] = short(acc, i, 0, taps[0]).astype(BF16)


def gate_kernel(query, returned, out):
    for group in range(4):
        mixed = returned[:, group].astype(F32).reshape(128, BLOCK).T
        out[group] = (query[group].astype(F32) * mixed).astype(BF16)


def order_kernel(gated, out):
    cols = jnp.concatenate([gated[g] for g in range(4)], axis=1)
    out[...] = dot(cols, order_table(False)).astype(BF16)


def call(kernel, out_shape, args, scratch=(), in_specs=None, flops=10**8):
    whole = pl.BlockSpec(memory_space=pltpu.VMEM)
    specs = in_specs or [whole] * len(args)
    moved = sum(math.prod(a.shape) * a.dtype.itemsize for a in args)
    return pl.pallas_call(
        kernel,
        out_shape=out_shape,
        in_specs=specs,
        out_specs=jax.tree.map(lambda _: whole, out_shape),
        scratch_shapes=list(scratch),
        compiler_params=pltpu.CompilerParams(vmem_limit_bytes=20 * 2**20),
        cost_estimate=pl.CostEstimate(flops=flops, bytes_accessed=moved, transcendentals=0),
    )(*args)


def of_previous(value, axes):
    count = math.prod(SIZES[AXES.index(a)] for a in axes)
    return lax.ppermute(value, axes, [(i, i + 1) for i in range(count - 1)])


def swapped(value, axes, bits):
    count = math.prod(SIZES[AXES.index(a)] for a in axes)
    return lax.ppermute(value, axes, [(i, i ^ bits) for i in range(count)])


def mixer(tokens, w_query, w_key, w_value, short_taps, filters, skip_gain):
    shape = jax.ShapeDtypeStruct
    whole = pl.BlockSpec(memory_space=pltpu.VMEM)
    smem = pl.BlockSpec(memory_space=pltpu.SMEM)
    place = lax.axis_index(AXES)
    core, z_lo, yl, x, z_hi = place % 2, place // 2 % 4, place // 8 % 2, place // 64 % 4, place // 256
    where = jnp.stack([z_hi * 4 + z_lo, core, z_hi * 2 + yl, z_hi, x])

    anywhere = pl.BlockSpec(memory_space=pl.ANY)
    halo = of_previous(tokens[-HALO:], TOK)
    part = shape((2, 3, 64, 128), BF16)
    own, others = call(
        weights_kernel,
        (part, part),
        (where, *(pltpu.with_memory_space_constraint(w, pltpu.HBM) for w in (w_key, w_value, w_query))),
        (pltpu.VMEM((3, 64, 512), BF16), pltpu.SemaphoreType.DMA((3,))),
        in_specs=[smem] + [anywhere] * 3,
    )
    got = swapped(others, ("z_hi",), 1)
    first = from_everyone(jnp.stack([own, got], axis=2), ("yh",), ("yl",))

    ring = ("z_hi", "z_lo")
    mine = jnp.concatenate([halo, tokens], axis=0)[None]
    far_block = swapped(mine, ring, 4)
    two = jnp.concatenate([mine, far_block], axis=0)
    next_two = swapped(two, ring, 2)
    taps = short_taps.reshape(3, 3, 2, 16, 2, 8)
    taps = lax.dynamic_index_in_dim(taps, z_hi, 2, keepdims=False)
    taps = lax.dynamic_index_in_dim(taps, yl, 3, keepdims=False).reshape(3, 3, 128)

    first, taps, where = lax.optimization_barrier((first, taps, where))
    weights = from_everyone(first[:, :2], ("x",))
    ours = [two, next_two]
    for _ in range(2):
        ours.append(swapped(ours[len(ours) - 2], ring, 1))
    features = list(ours)
    for pair in ours:
        features.append(swapped(pair, ("yl",), 1))
    for pair in tuple(features):
        features.append(swapped(pair, ("core",), 1))
    slice_of_first, last = lax.optimization_barrier((first[:, 2], features[-1]))
    features = (*features[:-1], last)
    query_weights = [slice_of_first]
    query_weights += [swapped(query_weights[0], ("x",), d) for d in (1, 2, 3)]

    kept = [pltpu.with_memory_space_constraint(v, pltpu.HBM) for v in features]
    blocks = [pltpu.VMEM((2, ROWS, 512), BF16)] * 16
    key_value = call(
        key_value_kernel,
        shape((16, 4, 8, BLOCK), BF16),
        (where, weights, *kept, taps),
        [pltpu.VMEM((4, 8, 2, 2, 64, 128), BF16)]
        + blocks
        + [pltpu.VMEM((4 * ROWS, 256), F32), pltpu.SemaphoreType.DMA((20,))],
        in_specs=[smem] + [anywhere] * 17 + [whole],
        flops=2 * 544 * 4096 * 256,
    )
    owned = exchanged(key_value, ("x", "yh"))
    tables, turns = dft_tables()
    filters, _ = lax.optimization_barrier((filters, key_value))
    spec, tables, turns = call(
        filter_kernel,
        (shape((8 * POINTS, 2 * POINTS), F32), shape(tables.shape, BF16), shape(turns.shape, F32)),
        (filters, tables, turns),
        (pltpu.VMEM((512, POINTS), F32),),
    )
    owned, spec = lax.optimization_barrier((owned, spec))
    mixed = call(
        conv_kernel,
        shape((16, 2, 2, 8, BLOCK), BF16),
        (owned.reshape(16, 2, 2, 8, BLOCK), spec, skip_gain, tables, turns),
        (pltpu.VMEM((512, POINTS), F32), pltpu.VMEM((512, POINTS), F32)),
        in_specs=[whole, whole, smem, whole, whole],
        flops=2 * 168 * 10**6,
    )
    returned = exchanged(mixed.reshape(16, 4, 8, BLOCK), ("x", "yh"))
    taps, _ = lax.optimization_barrier((taps, mixed))
    query = call(
        query_kernel,
        shape((4, BLOCK, 128), BF16),
        (where, *query_weights, *kept, taps),
        [pltpu.VMEM((4, 8, 2, 64, 128), BF16)]
        + blocks
        + [pltpu.VMEM((4 * ROWS, 128), F32), pltpu.SemaphoreType.DMA((20,))],
        in_specs=[smem] + [anywhere] * 20 + [whole],
        flops=2 * 544 * 4096 * 128,
    )
    gated = call(gate_kernel, shape((4, BLOCK, 128), BF16), (query, returned))
    gated = exchanged(gated, ("z_hi", "yl"))
    return call(order_kernel, shape((BLOCK, 512), BF16), (gated,))


def solution(mesh):
    fine = Mesh(mesh.devices.reshape(SIZES), AXES)
    in_specs = (
        P(TOK, TP),
        P(TOK, TP),
        P(TOK, TP),
        P(TOK, TP),
        P(None, None, TP),
        P(TP + TOK, None),
        P(TP + TOK),
    )
    return jax.shard_map(mixer, mesh=fine, in_specs=in_specs, out_specs=P(TOK, TP), check_vma=False)
```

```python
import math

import jax
import jax.numpy as jnp
import numpy as np
from jax import lax
from jax.experimental import pallas as pl
from jax.experimental.pallas import tpu as pltpu
from jax.sharding import Mesh
from jax.sharding import PartitionSpec as P

AXES = ("z_hi", "x", "yh", "yl", "z_lo", "core")
SIZES = (2, 4, 4, 2, 4, 2)
TOK = AXES[:4]
TP = AXES[4:]
HALO = 8
BLOCK = 128
ROWS = HALO + BLOCK
POINTS = 128
F32 = jnp.float32
BF16 = jnp.bfloat16


def exchanged(value, axes):
    return lax.all_to_all(value, axes, split_axis=0, concat_axis=0, tiled=True)


def from_everyone(value, axes, apart=()):
    count = math.prod(SIZES[AXES.index(a)] for a in axes)
    copies = jnp.broadcast_to(value, (count, *value.shape))
    if apart:
        copies = copies.reshape(-1, *value.shape[1:])
    return exchanged(copies, axes + apart)


def dft_tables():
    n = np.arange(POINTS)
    full = 2.0 * np.pi * (np.outer(n, n) % POINTS) / POINTS
    cos, sin = np.cos(full), np.sin(full)
    half = POINTS // 2
    outer = np.concatenate([cos, -sin], axis=0)
    outer = np.concatenate([outer, outer], axis=1)
    inner = np.block([[cos, -sin], [sin, cos]])
    back_inner = np.block([[cos, sin], [-sin, cos]])
    back_outer = np.concatenate([cos[:half], -sin[:half]], axis=1) / POINTS**2
    twist = 2.0 * np.pi * np.outer(n, n) / POINTS**2
    tables = np.concatenate([inner, back_inner, outer, back_outer], axis=0)
    turns = np.concatenate([np.cos(twist), np.sin(twist)], axis=0)
    return jnp.asarray(tables, F32).astype(BF16), jnp.asarray(turns, F32)


def dot(a, b):
    return jnp.dot(a, b, preferred_element_type=F32)


def spectrum(rows, tables, turns):
    cos, sin = turns[0:POINTS], turns[POINTS:]
    blocks = jnp.concatenate(
        [rows[pl.ds(c, 64, stride=8), :].astype(BF16) for c in range(8)], axis=1
    )
    first = dot(tables[512:768, 0:64], blocks)
    turned = []
    for c in range(8):
        re = first[:POINTS, c * POINTS : (c + 1) * POINTS]
        im = first[POINTS:, c * POINTS : (c + 1) * POINTS]
        turned.append(
            jnp.concatenate([re * cos + im * sin, im * cos - re * sin], axis=1).astype(BF16)
        )
    return dot(jnp.concatenate(turned, axis=0), tables[0:256])


def filter_kernel(filters, tables, turns, spec, tables_out, turns_out, rows):
    tables_out[...] = tables[...]
    turns_out[...] = turns[...]
    taps = filters[...]
    unit = taps / jnp.sqrt(jnp.sum(taps * taps, axis=1, keepdims=True) + 1e-06)
    for b in range(64):
        rows[pl.ds(b * 8, 8), :] = unit[:, b * POINTS : (b + 1) * POINTS]
    spec[...] = spectrum(rows, tables, turns)


def conv_kernel(signal, spec, skip, tables, turns, mixed, rows, out):
    for z in range(2):
        rows[pl.ds(z * 256, 256), :] = signal[:, z].astype(F32).reshape(256, POINTS)
    cos, sin = turns[0:POINTS], turns[POINTS:]
    sig = spectrum(rows, tables, turns)
    re, im = sig[:, :POINTS], sig[:, POINTS:]
    f_re, f_im = spec[:, :POINTS], spec[:, POINTS:]
    prod = jnp.concatenate([re * f_re - im * f_im, re * f_im + im * f_re], axis=1)
    back = dot(prod.astype(BF16), tables[256:512])
    turned = []
    for c in range(8):
        b_re = back[c * POINTS : (c + 1) * POINTS, :POINTS]
        b_im = back[c * POINTS : (c + 1) * POINTS, POINTS:]
        turned.append(
            jnp.concatenate([b_re * cos - b_im * sin, b_re * sin + b_im * cos], axis=0).astype(BF16)
        )
    result = dot(tables[768:832], jnp.concatenate(turned, axis=1))
    for c in range(8):
        piece = result[:, c * POINTS : (c + 1) * POINTS]
        out[pl.ds(c, 64, stride=8), :] = piece + skip[c] * rows[pl.ds(c, 64, stride=8), :]
    for z in range(2):
        mixed[:, z] = out[pl.ds(z * 256, 256), :].astype(BF16).reshape(16, 2, 8, POINTS)


def order_table(rows_are_natural):
    shape = (512, 512)
    row = lax.broadcasted_iota(jnp.int32, shape, 0)
    col = lax.broadcasted_iota(jnp.int32, shape, 1)
    grouped, natural = (col, row) if rows_are_natural else (row, col)
    quarter, xy, j = grouped // 128, (grouped // 8) % 16, grouped % 8
    place = (quarter // 2) * 256 + xy * 16 + (quarter % 2) * 8 + j
    return (natural == place).astype(F32).astype(BF16)


def weights_kernel(where, w_key, w_value, w_query, mine, theirs, held, sems):
    copies = fetched((w_key, w_value, w_query), [held.at[p] for p in range(3)], sems)
    table = order_table(True)
    lower = where[2] < 2
    for p in range(3):
        copies[p].wait()
        cols = dot(held[p], table)
        ours = jnp.where(lower, cols[:, :256], cols[:, 256:]).astype(BF16)
        others = jnp.where(lower, cols[:, 256:], cols[:, :256]).astype(BF16)
        for yl in range(2):
            mine[yl, p] = ours[:, yl * 128 : (yl + 1) * 128]
            theirs[yl, p] = others[:, yl * 128 : (yl + 1) * 128]


def fetched(sources, held, sems):
    copies = [pltpu.make_async_copy(a, b, sems.at[i]) for i, (a, b) in enumerate(zip(sources, held))]
    for copy in copies:
        copy.start()
    return copies


def projected(where, features, w, acc, ready):
    for i, (half, low) in enumerate((h, l) for h in range(2) for l in (0, 2, 1, 3)):
        if i % 2 == 0:
            for copy in ready(i // 2):
                copy.wait()
        pieces = [
            features[half * 4 + parity * 2 + low % 2][(low // 2) * 2 : (low // 2) * 2 + 2]
            for parity in range(2)
        ]
        rows = jnp.concatenate([p.reshape(2 * ROWS, 512) for p in pieces], axis=0)
        term = dot(rows, w(i // 2, part_of(where, half, low)))
        if i == 0:
            acc[...] = term
        else:
            acc[...] += term


def part_of(where, half, low):
    return ((where[0] ^ low) & 3) * 2 + (where[1] ^ half)


def group_of(where, i):
    return ((i % 2) * 2 + i // 2) ^ where[2]


def short(acc, group, at, taps):
    top = group * ROWS + HALO
    cols = pl.ds(at, 128)
    return (
        taps[0:1] * acc[pl.ds(top, BLOCK), cols]
        + taps[1:2] * acc[pl.ds(top - 1, BLOCK), cols]
        + taps[2:3] * acc[pl.ds(top - 2, BLOCK), cols]
    )


def key_value_kernel(where, *refs):
    sources, (taps, out), (w, *held), (acc, sems) = refs[:9], refs[9:11], refs[11:20], refs[20:]
    pairs = [(half, low) for half in range(2) for low in range(2)]
    columns = [sources[0].at[part_of(where, half, low) & 3] for half, low in pairs]
    order = [half * 4 + parity * 2 + low for half, low in pairs for parity in range(2)]
    froms, targets = [], []
    for j in range(4):
        froms += [columns[j], sources[1 + order[2 * j]], sources[1 + order[2 * j + 1]]]
        targets += [w.at[j], held[order[2 * j]], held[order[2 * j + 1]]]
    copies = fetched(froms, targets, sems)

    def weights(j, part):
        z_hi = (part >> 2) ^ where[3]
        return jnp.concatenate([w[j, :, p, z_hi].reshape(512, 128) for p in range(2)], axis=1)

    projected(where, held, weights, acc, lambda j: copies[3 * j : 3 * j + 3])
    for i in range(4):
        keyed = short(acc, i, 0, taps[1])
        valued = short(acc, i, 128, taps[2])
        out[:, group_of(where, i)] = (keyed * valued).T.reshape(16, 8, BLOCK).astype(BF16)


def query_kernel(where, *refs):
    sources, (taps, out), (w, *held), (acc, sems) = refs[:12], refs[12:14], refs[14:23], refs[23:]
    copies = fetched(sources, [w.at[d] for d in range(4)] + held, sems)

    def weights(j, part):
        return w[(part & 3) ^ where[4], :, (part >> 2) ^ where[3]].reshape(512, 128)

    projected(where, held, weights, acc, lambda j: copies if j == 0 else [])
    for i in range(4):
        out[group_of(where, i)] = short(acc, i, 0, taps[0]).astype(BF16)


def gate_kernel(query, returned, out):
    for group in range(4):
        mixed = returned[:, group].astype(F32).reshape(128, BLOCK).T
        out[group] = (query[group].astype(F32) * mixed).astype(BF16)


def order_kernel(gated, out):
    cols = jnp.concatenate([gated[g] for g in range(4)], axis=1)
    out[...] = dot(cols, order_table(False)).astype(BF16)


def call(kernel, out_shape, args, scratch=(), in_specs=None, flops=10**8):
    whole = pl.BlockSpec(memory_space=pltpu.VMEM)
    specs = in_specs or [whole] * len(args)
    moved = sum(math.prod(a.shape) * a.dtype.itemsize for a in args)
    return pl.pallas_call(
        kernel,
        out_shape=out_shape,
        in_specs=specs,
        out_specs=jax.tree.map(lambda _: whole, out_shape),
        scratch_shapes=list(scratch),
        compiler_params=pltpu.CompilerParams(vmem_limit_bytes=20 * 2**20),
        cost_estimate=pl.CostEstimate(flops=flops, bytes_accessed=moved, transcendentals=0),
    )(*args)


def of_previous(value, axes):
    count = math.prod(SIZES[AXES.index(a)] for a in axes)
    return lax.ppermute(value, axes, [(i, i + 1) for i in range(count - 1)])


def swapped(value, axes, bits):
    count = math.prod(SIZES[AXES.index(a)] for a in axes)
    return lax.ppermute(value, axes, [(i, i ^ bits) for i in range(count)])


def mixer(tokens, w_query, w_key, w_value, short_taps, filters, skip_gain):
    shape = jax.ShapeDtypeStruct
    whole = pl.BlockSpec(memory_space=pltpu.VMEM)
    smem = pl.BlockSpec(memory_space=pltpu.SMEM)
    place = lax.axis_index(AXES)
    core, z_lo, yl, x, z_hi = place % 2, place // 2 % 4, place // 8 % 2, place // 64 % 4, place // 256
    where = jnp.stack([z_hi * 4 + z_lo, core, z_hi * 2 + yl, z_hi, x])

    anywhere = pl.BlockSpec(memory_space=pl.ANY)
    halo = of_previous(tokens[-HALO:], TOK)
    part = shape((2, 3, 64, 128), BF16)
    own, others = call(
        weights_kernel,
        (part, part),
        (where, *(pltpu.with_memory_space_constraint(w, pltpu.HBM) for w in (w_key, w_value, w_query))),
        (pltpu.VMEM((3, 64, 512), BF16), pltpu.SemaphoreType.DMA((3,))),
        in_specs=[smem] + [anywhere] * 3,
    )
    others, halo = lax.optimization_barrier((others, halo))
    got = swapped(others, ("z_hi",), 1)
    first = from_everyone(jnp.stack([own, got], axis=2), ("yh",), ("yl",))

    ring = ("z_hi", "z_lo")
    mine = jnp.concatenate([halo, tokens], axis=0)[None]
    far_block = swapped(mine, ring, 4)
    two = jnp.concatenate([mine, far_block], axis=0)
    even = jnp.concatenate([two, swapped(two, ring, 2)], axis=0)
    taps = short_taps.reshape(3, 3, 2, 16, 2, 8)
    taps = lax.dynamic_index_in_dim(taps, z_hi, 2, keepdims=False)
    taps = lax.dynamic_index_in_dim(taps, yl, 3, keepdims=False).reshape(3, 3, 128)

    first, taps, where, _ = lax.optimization_barrier((first, taps, where, even))
    weights = from_everyone(first[:, :2], ("x",))
    odd = swapped(even, ring, 1)
    even_y = swapped(even, ("yl",), 1)
    odd_y = swapped(odd, ("yl",), 1)
    ours = (even, odd, even_y, odd_y)
    features = [swapped(v, ("core",), 1) for v in ours]
    features = (*ours, *features)
    query_weights = [first[:, 2]]
    query_weights += [swapped(query_weights[0], ("x",), d) for d in (1, 2, 3)]

    kept = [pltpu.with_memory_space_constraint(v, pltpu.HBM) for v in features]
    blocks = [pltpu.VMEM((4, ROWS, 512), BF16)] * 8
    key_value = call(
        key_value_kernel,
        shape((16, 4, 8, BLOCK), BF16),
        (where, weights, *kept, taps),
        [pltpu.VMEM((4, 8, 2, 2, 64, 128), BF16)]
        + blocks
        + [pltpu.VMEM((4 * ROWS, 256), F32), pltpu.SemaphoreType.DMA((12,))],
        in_specs=[smem] + [anywhere] * 9 + [whole],
        flops=2 * 544 * 4096 * 256,
    )
    owned = exchanged(key_value, ("x", "yh"))
    tables, turns = dft_tables()
    filters, _ = lax.optimization_barrier((filters, key_value))
    spec, tables, turns = call(
        filter_kernel,
        (shape((8 * POINTS, 2 * POINTS), F32), shape(tables.shape, BF16), shape(turns.shape, F32)),
        (filters, tables, turns),
        (pltpu.VMEM((512, POINTS), F32),),
    )
    owned, spec = lax.optimization_barrier((owned, spec))
    mixed = call(
        conv_kernel,
        shape((16, 2, 2, 8, BLOCK), BF16),
        (owned.reshape(16, 2, 2, 8, BLOCK), spec, skip_gain, tables, turns),
        (pltpu.VMEM((512, POINTS), F32), pltpu.VMEM((512, POINTS), F32)),
        in_specs=[whole, whole, smem, whole, whole],
        flops=2 * 168 * 10**6,
    )
    returned = exchanged(mixed.reshape(16, 4, 8, BLOCK), ("x", "yh"))
    taps, _ = lax.optimization_barrier((taps, mixed))
    query = call(
        query_kernel,
        shape((4, BLOCK, 128), BF16),
        (where, *query_weights, *kept, taps),
        [pltpu.VMEM((4, 8, 2, 64, 128), BF16)]
        + blocks
        + [pltpu.VMEM((4 * ROWS, 128), F32), pltpu.SemaphoreType.DMA((12,))],
        in_specs=[smem] + [anywhere] * 12 + [whole],
        flops=2 * 544 * 4096 * 128,
    )
    gated = call(gate_kernel, shape((4, BLOCK, 128), BF16), (query, returned))
    gated = exchanged(gated, ("z_hi", "yl"))
    return call(order_kernel, shape((BLOCK, 512), BF16), (gated,))


def solution(mesh):
    fine = Mesh(mesh.devices.reshape(SIZES), AXES)
    in_specs = (
        P(TOK, TP),
        P(TOK, TP),
        P(TOK, TP),
        P(TOK, TP),
        P(None, None, TP),
        P(TP + TOK, None),
        P(TP + TOK),
    )
    return jax.shard_map(mixer, mesh=fine, in_specs=in_specs, out_specs=P(TOK, TP), check_vma=False)
```
